128 devices in a mesh: nodes: 16 (over x_hi, y, core), feat: 8 (over x_lo, z).
Axes of the slice: x: 4 (x_hi: 2, x_lo: 2; x = x_hi * 2 + x_lo), y: 4, z: 4, core: 2. Of those that a mesh axis runs over, the one named last changes fastest.
Arguments:
- feats: bfloat16 [131072, 128], P('nodes', 'feat'), may hold values from -6 to 6
- tiles: bfloat16 [16, 16, 32, 128, 128], P('nodes'), may hold values from -0.25 to 0.25
- dst_block: int32 [16, 16, 32], P('nodes'), may hold values from 0 to 63
- src_block: int32 [16, 16, 32], P('nodes'), may hold values from 0 to 63
- tile_counts: int32 [16, 16], P('nodes'), may hold values from 1 to 32, as said below
- norm: float32 [131072], P('nodes'), may hold values from 0.3 to 3
- weight: bfloat16 [128, 256], P('feat'), may hold values from -0.5 to 0.5
- bias: float32 [256], P('feat'), may hold values from -3 to 3
- cotangent: bfloat16 [131072, 256], P('nodes', 'feat'), may hold values from -6 to 6
Outputs:
- hidden: bfloat16 [131072, 256], P('nodes', 'feat')
- grad_weight: float32 [128, 256], P('feat')
- grad_bias: float32 [256], P('feat')
- grad_feats: float32 [131072, 128], P('nodes', 'feat')
The draws below stay inside these ranges and needn't reach their ends.
Inputs may be any that keep to these rules, and one draw needn't show every extreme that they name: Slots at or past tile_counts[o, p] hold no tile; one source slab has 32 tiles from every owner slab in every draw.
All inputs are finite; a program needn't handle non-finite values.
Results may differ from the reference program's by a relative error of at most 0.0075.
Values may be sent and summed in bfloat16 or wider, within the bound.
No kernel may reach another device: no remote copies, remote signals or barrier semaphores. Data moves between devices by JAX's collectives and lax.ppermute only.
A program may use at most 128 MiB of HBM per device.

```python
import math
import jax
import jax.numpy as jnp
from jax import lax

FIN = 128
HID = 256
TILE = 128
BLK = 64
CAP = 32
SLABS = 16
NODES = 131072


def draw_tile_counts(key, part):
    level_key, drawn_key, column_key = jax.random.split(key, 3)
    level = jax.random.randint(level_key, (SLABS, 1), 0, 4)
    drawn = jax.random.randint(drawn_key, (SLABS, SLABS), 1, CAP + 1)
    counts = jnp.clip(drawn - (3 - level) * CAP // 8, 1, CAP)
    column = jax.random.randint(column_key, (), 0, SLABS)
    filled = jnp.where(jnp.arange(SLABS)[None, :] == column, CAP, counts)
    return filled.astype(jnp.int32)


def touch_ends(values, own_key, least, high):
    longest = values.shape.index(max(values.shape))
    spots = []
    for shift in (0, 1):
        where = [jax.random.randint(jax.random.fold_in(own_key, axis), (), 0, length) for axis, length in enumerate(values.shape)]
        where[longest] = (where[longest] + shift) % values.shape[longest]
        spots.append(tuple(where))
    return values.at[spots[0]].set(least).at[spots[1]].set(high)


def steps_of(key, dims, cuts, least, top_value):
    gain = 1.0
    for axis_at, blocks in cuts:
        steps = jax.random.uniform(jax.random.fold_in(jax.random.fold_in(key, 6), axis_at), (blocks,), jnp.float32, least / len(cuts), top_value / len(cuts))
        gain = gain * jnp.repeat(jnp.exp(steps), dims[axis_at] // blocks).reshape((-1,) + (1,) * (len(dims) - 1 - axis_at))
    return gain


def scatter_about(key, dims, scale, bound, pieces=(), kind=jnp.bfloat16):
    values = scale * jax.random.normal(key, dims, jnp.float32)
    if pieces:
        values = values * steps_of(key, dims, pieces, -0.22, 0.18)
    return jnp.clip(values, -bound, bound).astype(kind)


def setup_inputs(seed: int = 0) -> dict:
    splits = jax.random.split(jax.random.key(seed), 10)
    feats = scatter_about(splits[0], (NODES, FIN), 1.0, 6.0, ((0, 16), (1, 8)))
    tiles = scatter_about(splits[1], (SLABS, SLABS, CAP, TILE, TILE), (TILE * SLABS * CAP // (2 * BLK)) ** -0.5, 0.25, ((0, 16),))
    dst_block = touch_ends(jax.random.randint(splits[2], (SLABS, SLABS, CAP), 0, BLK), jax.random.fold_in(splits[2], 1), 0, BLK - 1).astype(jnp.int32)
    src_block = touch_ends(jax.random.randint(splits[3], (SLABS, SLABS, CAP), 0, BLK), jax.random.fold_in(splits[3], 1), 0, BLK - 1).astype(jnp.int32)
    tile_counts = draw_tile_counts(jax.random.fold_in(splits[9], 71), 0)
    norm = jnp.clip(jnp.exp(math.log(3.0) - 2.3025851 * jax.random.uniform(splits[5], (NODES,), jnp.float32) ** steps_of(splits[5], (NODES,), ((0, 16),), -0.2, 0.2)), 0.3, 3.0)
    weight = scatter_about(splits[6], (FIN, HID), FIN ** -0.5, 0.5, ((0, 8),))
    bias = scatter_about(splits[7], (HID,), 0.5, 3.0, ((0, 8),), jnp.float32)
    cotangent = scatter_about(splits[8], (NODES, HID), 1.0, 6.0, ((0, 16), (1, 8)))
    return {"feats": feats, "tiles": tiles, "dst_block": dst_block, "src_block": src_block, "tile_counts": tile_counts, "norm": norm, "weight": weight, "bias": bias, "cotangent": cotangent}


def reference(feats, tiles, dst_block, src_block, tile_counts, norm, weight, bias, cotangent):
    highest = lax.Precision.HIGHEST
    scaled = (norm[:, None] * feats.astype(jnp.float32)).astype(jnp.bfloat16)
    scaled_blocks = scaled.reshape(SLABS, BLK, TILE, FIN)
    slot_ids = jnp.arange(CAP, dtype=jnp.int32)
    block_ids = jnp.arange(BLK, dtype=jnp.int32)
    peer_ids = jnp.arange(SLABS, dtype=jnp.int32)

    def forward_owner(owner):
        tile_set = tiles[owner].astype(jnp.float32)
        picked = scaled_blocks[peer_ids[:, None], src_block[owner]].astype(jnp.float32)
        product = jnp.einsum("pcij,pcjf->pcif", tile_set, picked, precision=highest)
        usable = (slot_ids[None, :] < tile_counts[owner][:, None]).astype(jnp.float32)
        placing = (dst_block[owner][..., None] == block_ids).astype(jnp.float32) * usable[..., None]
        return jnp.einsum("pcb,pcif->bif", placing, product, precision=highest)

    summed = lax.map(forward_owner, peer_ids)
    aggregated = (norm[:, None] * summed.reshape(NODES, FIN)).astype(jnp.bfloat16)
    pre = jnp.dot(aggregated, weight, preferred_element_type=jnp.float32) + bias
    hidden = jax.nn.silu(pre).astype(jnp.bfloat16)
    sigma = jax.nn.sigmoid(pre)
    grad_pre = (cotangent.astype(jnp.float32) * sigma * (1.0 + pre * (1.0 - sigma))).astype(jnp.bfloat16)
    scale = NODES ** -0.5
    grad_weight = jnp.dot(aggregated.T, grad_pre, preferred_element_type=jnp.float32) * scale
    grad_bias = jnp.sum(grad_pre.astype(jnp.float32), axis=0) * scale
    back_scaled = (norm[:, None] * jnp.dot(grad_pre, weight.T, preferred_element_type=jnp.float32)).astype(jnp.bfloat16)
    back_blocks = back_scaled.reshape(SLABS, BLK, TILE, FIN)

    def backward_owner(carry, owner):
        tile_set = tiles[owner].astype(jnp.float32)
        picked = back_blocks[owner][dst_block[owner]].astype(jnp.float32)
        usable = (slot_ids[None, :] < tile_counts[owner][:, None]).astype(jnp.float32)
        partial_back = jnp.einsum("pcij,pcif->pcjf", tile_set, picked, precision=highest) * usable[:, :, None, None]
        placing = (src_block[owner][..., None] == block_ids).astype(jnp.float32)
        return carry + jnp.einsum("pcb,pcjf->pbjf", placing, partial_back, precision=highest), None

    start_total = jnp.zeros((SLABS, BLK, TILE, FIN), jnp.float32)
    returned, unused = lax.scan(backward_owner, start_total, peer_ids)
    grad_feats = norm[:, None] * returned.reshape(NODES, FIN)
    return hidden, grad_weight, grad_bias, grad_feats
```

```python
import functools

import jax
import jax.numpy as jnp
from jax import lax
from jax.experimental import pallas as pl
from jax.experimental.pallas import tpu as pltpu
from jax.sharding import PartitionSpec as P

LANES = 128
UNROLL = 8
BF16 = jnp.bfloat16
F32 = jnp.float32


def vmem(*shape):
    return pl.BlockSpec(memory_space=pltpu.VMEM)


def smem():
    return pl.BlockSpec(memory_space=pltpu.SMEM)


def hbm():
    return pl.BlockSpec(memory_space=pl.ANY)


def prepare_kernel(feats, norm, cotangent, weight, bias, scaled, payload):
    blocks = scaled.shape[0]
    peers, slots = payload.shape[0], payload.shape[1]
    per_peer = blocks // peers
    for b in range(blocks):
        lanes = pl.ds(b * LANES, LANES)
        scaled[b] = (norm[pl.ds(b, 1), :] * feats[:, lanes].astype(F32)).astype(BF16)
        payload[b // per_peer, b % per_peer] = cotangent[:, lanes]
    w = jnp.concatenate([weight[:, :LANES], weight[:, LANES:]], axis=0)
    rest = bias[...]
    parts = []
    for _ in range(3):
        part = rest.astype(BF16)
        rest = rest - part.astype(F32)
        parts.append(part.astype(F32))
    row = lax.broadcasted_iota(jnp.int32, (payload.shape[2], LANES), 0)
    packed = jnp.where(row == 0, parts[0], jnp.where(row == 1, parts[1], jnp.where(row == 2, parts[2], 0.0)))
    packed = packed.astype(BF16)
    for g in range(peers):
        payload[g, per_peer] = w
        payload[g, per_peer + 1] = packed


def start_tiles(slabs, counts, tiles, buffer, sems, pieces):
    slots = tiles.shape[1]
    for k in range(pieces):
        slab = slabs[k]
        count = counts[slab]
        for chunk in range(slots // UNROLL):
            @pl.when(chunk * UNROLL < count)
            def _():
                pltpu.make_async_copy(
                    tiles.at[slab, pl.ds(chunk * UNROLL, UNROLL)],
                    buffer.at[k, pl.ds(chunk * UNROLL, UNROLL)],
                    sems.at[k, chunk],
                ).start()


def over_tiles(k, slab, count, tiles, buffer, sems, source_of, target_of, dims, accumulator):
    def step(chunk, carry):
        first = chunk * UNROLL
        pltpu.make_async_copy(
            tiles.at[slab, pl.ds(first, UNROLL)], buffer.at[k, pl.ds(first, UNROLL)], sems.at[k, chunk]
        ).wait()
        products = []
        for j in range(UNROLL):
            c = first + j
            r = lax.dot_general(source_of(c), buffer[k, c], (dims, ((), ())), preferred_element_type=F32)
            products.append(jnp.where(c < count, r, 0.0))
        for j in range(UNROLL):
            t = target_of(first + j)
            accumulator[t] = accumulator[t] + products[j]
        return carry

    lax.fori_loop(0, (count + UNROLL - 1) // UNROLL, step, 0)


def forward_kernel(pieces, first, last, slabs, counts, src, dst, *refs):
    refs = list(refs)
    xs = [refs.pop(0) for _ in range(pieces)]
    tiles = refs.pop(0)
    start = None if first else refs.pop(0)
    norm = refs.pop(0) if last else None
    out, buffer, sems = refs[0], refs[1], refs[2]
    acc = refs[3] if last else out
    start_tiles(slabs, counts, tiles, buffer, sems, pieces)
    for b in range(acc.shape[0]):
        acc[b] = jnp.zeros(acc.shape[1:], F32) if first else start[b]
    for k in range(pieces):
        slab = slabs[k]
        over_tiles(
            k, slab, counts[slab], tiles, buffer, sems,
            lambda c, slab=slab, k=k: xs[k][src[slab, c]],
            lambda c, slab=slab: dst[slab, c],
            ((1,), (1,)), acc,
        )
    if last:
        per_peer = out.shape[1]
        for b in range(acc.shape[0]):
            out[b // per_peer, b % per_peer] = (norm[pl.ds(b, 1), :] * acc[b]).astype(BF16)


def forward_call(xs, slabs, counts, src, dst, tiles, start, norm, peers):
    pieces = len(xs)
    first, last = start is None, norm is not None
    shape = xs[0].shape
    args = [slabs, counts, src, dst, *xs, tiles]
    specs = [smem()] * 4 + [vmem()] * pieces + [hbm()]
    if not first:
        args.append(start)
        specs.append(vmem())
    scratch = [
        pltpu.VMEM((pieces, *tiles.shape[1:]), BF16),
        pltpu.SemaphoreType.DMA((pieces, tiles.shape[1] // UNROLL)),
    ]
    if last:
        args.append(norm)
        specs.append(vmem())
        scratch.append(pltpu.VMEM(shape, F32))
        out = jax.ShapeDtypeStruct((peers, shape[0] // peers, *shape[1:]), BF16)
    else:
        out = jax.ShapeDtypeStruct(shape, F32)
    return pl.pallas_call(
        functools.partial(forward_kernel, pieces, first, last),
        out_shape=out, in_specs=specs, out_specs=vmem(), scratch_shapes=scratch,
        name="forward_tiles",
    )(*args)


def backward_kernel(pieces, added, kept, slabs, counts, src, dst, *refs):
    refs = list(refs)
    ys = refs.pop(0)
    tiles = refs.pop(0)
    adds = [refs.pop(0) for _ in range(pieces)] if added else None
    outs = [refs.pop(0) for _ in range(pieces)]
    buffer, sems, acc = refs
    per_peer = ys.shape[1]
    blocks = acc.shape[0]
    start_tiles(slabs, counts, tiles, buffer, sems, pieces)
    for k in range(pieces):
        slab = slabs[k]
        for b in range(blocks):
            acc[b] = adds[k][b].astype(F32) if added else jnp.zeros(acc.shape[1:], F32)

        def source_of(c, slab=slab):
            d = dst[slab, c]
            return ys[d // per_peer, d % per_peer]

        over_tiles(
            k, slab, counts[slab], tiles, buffer, sems, source_of,
            lambda c, slab=slab: src[slab, c], ((1,), (0,)), acc,
        )
        for b in range(blocks):
            outs[k][b] = acc[b].astype(outs[k].dtype)


def backward_call(ys, slabs, counts, src, dst, tiles, adds, kept, pieces):
    blocks = ys.shape[0] * ys.shape[1]
    shape = (blocks, *ys.shape[2:])
    added = adds is not None
    args = [slabs, counts, src, dst, ys, tiles] + (list(adds) if added else [])
    specs = [smem()] * 4 + [vmem(), hbm()] + [vmem()] * (pieces if added else 0)
    outs = [jax.ShapeDtypeStruct(shape, F32 if k == kept else BF16) for k in range(pieces)]
    return pl.pallas_call(
        functools.partial(backward_kernel, pieces, added, kept),
        out_shape=outs, in_specs=specs, out_specs=[vmem()] * pieces,
        scratch_shapes=[
            pltpu.VMEM((pieces, *tiles.shape[1:]), BF16),
            pltpu.SemaphoreType.DMA((pieces, tiles.shape[1] // UNROLL)),
            pltpu.VMEM(shape, F32),
        ],
        name="backward_tiles",
    )(*args)


def dense_kernel(place, agg, received, norm, hidden, back, grads):
    peers, blocks, feat_local = agg.shape[0], agg.shape[1], agg.shape[2]
    hid_local = hidden.shape[2]
    halves = received.shape[2] // feat_local
    weight = jnp.concatenate(
        [
            jnp.concatenate([received[g, blocks, pl.ds(h * feat_local, feat_local), :] for h in range(halves)], axis=1)
            for g in range(peers)
        ],
        axis=0,
    )
    bias_rows = []
    for g in range(peers):
        parts = received[g, blocks + 1].astype(F32)
        bias_rows.append((parts[0:1] + parts[1:2] + parts[2:3])[:, :hid_local])
    bias = jnp.concatenate(bias_rows, axis=1)
    bias = jnp.transpose(jnp.broadcast_to(bias, (8, bias.shape[1])))[:, 0:1]
    grad = jnp.zeros(grads.shape, F32)
    for b in range(blocks):
        agg_b = jnp.concatenate([agg[g, b] for g in range(peers)], axis=0)
        cot_b = jnp.concatenate([received[g, b] for g in range(peers)], axis=0).astype(F32)
        pre = lax.dot_general(weight, agg_b, (((0,), (0,)), ((), ())), preferred_element_type=F32) + bias
        sig = 1.0 / (1.0 + jnp.exp(-pre))
        hid = (pre * sig).astype(BF16)
        grad_pre = (cot_b * sig * (1.0 + pre * (1.0 - sig))).astype(BF16)
        back_b = jnp.dot(weight, grad_pre, preferred_element_type=F32)
        back_b = (norm[pl.ds(place[0] * blocks + b, 1), :] * back_b).astype(BF16)
        left = jnp.concatenate([agg_b, jnp.ones((8, LANES), BF16)], axis=0)
        grad = grad + lax.dot_general(left, grad_pre, (((1,), (1,)), ((), ())), preferred_element_type=F32)
        for g in range(peers):
            hidden[g, b] = hid[g * hid_local:(g + 1) * hid_local]
            back[g, b] = back_b[g * feat_local:(g + 1) * feat_local]
    grads[...] = grad


def finish_kernel(kept, norm, *refs):
    out = refs[-1]
    for b in range(kept.shape[0]):
        total = kept[b]
        for r in refs[:-1]:
            total = total + r[b].astype(F32)
        out[:, pl.ds(b * LANES, LANES)] = norm[pl.ds(b, 1), :] * total


def on_device(feats, tiles, dst_block, src_block, tile_counts, norm, weight, bias, cotangent):
    rows, feat_local = feats.shape
    tile = tiles.shape[-1]
    blocks = rows // tile
    hid = weight.shape[1]
    hid_local = cotangent.shape[1]
    peers = lax.axis_size("feat")
    slabs = lax.axis_size("nodes")
    per_peer = blocks // peers
    own_tiles, own_dst, own_src, own_counts = tiles[0], dst_block[0], src_block[0], tile_counts[0]
    norm_blocks = norm.reshape(blocks, tile)
    me = lax.axis_index("nodes")
    me_x, me_y, me_c = me // 8, (me // 2) % 4, me % 2
    place = lax.axis_index("feat").astype(jnp.int32).reshape(1)

    def slab_at(dx, dy, dc):
        return ((me_x + dx) % 2) * 8 + ((me_y + dy) % 4) * 2 + (me_c + dc) % 2

    def move(value, dx, dy, dc):
        pairs = []
        for i in range(slabs):
            x, y, c = i // 8, (i // 2) % 4, i % 2
            pairs.append((i, ((x + dx) % 2) * 8 + ((y + dy) % 4) * 2 + (c + dc) % 2))
        return lax.ppermute(value, "nodes", pairs)

    scaled, payload = pl.pallas_call(
        prepare_kernel,
        out_shape=(
            jax.ShapeDtypeStruct((blocks, feat_local, LANES), BF16),
            jax.ShapeDtypeStruct((peers, per_peer + 2, hid_local, LANES), BF16),
        ),
        name="prepare",
    )(
        feats.T, norm_blocks, cotangent.T, weight,
        jnp.pad(bias.reshape(1, hid_local), ((0, 0), (0, LANES - hid_local))),
    )
    hops = [(0, 0), (0, 1), (0, 3), (1, 0), (1, 1), (1, 3), (0, 2), (1, 2)]
    pieces = {}
    for dx, dy in hops:
        pieces[dx, dy] = scaled if (dx, dy) == (0, 0) else move(scaled, dx, dy, 0)
    received = lax.all_to_all(payload, "feat", 0, 0)
    start = None
    groups = [hops[:1], hops[1:4], hops[4:6], hops[6:]]
    for g, group in enumerate(groups):
        xs, ids = [], []
        for dx, dy in group:
            for dc in (0, 1):
                value = pieces[dx, dy]
                xs.append(move(value, 0, 0, 1) if dc else value)
                ids.append(slab_at(-dx, -dy, dc))
        start = forward_call(
            xs, jnp.stack(ids).astype(jnp.int32), own_counts, own_src, own_dst, own_tiles, start,
            norm_blocks if g == len(groups) - 1 else None, peers,
        )
    agg = lax.all_to_all(start, "feat", 0, 0)
    hidden, back, grads = pl.pallas_call(
        dense_kernel,
        out_shape=(
            jax.ShapeDtypeStruct((peers, per_peer, hid_local, LANES), BF16),
            jax.ShapeDtypeStruct((peers, per_peer, feat_local, LANES), BF16),
            jax.ShapeDtypeStruct((peers * feat_local + 8, hid), F32),
        ),
        in_specs=[smem(), vmem(), vmem(), vmem()],
        name="dense",
    )(place, agg, received, norm_blocks)
    back = lax.all_to_all(back, "feat", 0, 0)

    order = [(1, 2), (0, 2), (1, 1), (1, 3), (0, 1), (0, 3), (1, 0), (0, 0)]
    halves = [order[:4], order[4:]]
    swapped = []
    for half in halves:
        ids = jnp.stack([slab_at(dx, dy, 1) for dx, dy in half]).astype(jnp.int32)
        parts = backward_call(back, ids, own_counts, own_src, own_dst, own_tiles, None, None, len(half))
        swapped.append([move(p, 0, 0, 1) for p in parts])
    arrived, kept = [], None
    for half, adds in zip(halves, swapped):
        ids = jnp.stack([slab_at(dx, dy, 0) for dx, dy in half]).astype(jnp.int32)
        stay = half.index((0, 0)) if (0, 0) in half else None
        parts = backward_call(back, ids, own_counts, own_src, own_dst, own_tiles, adds, stay, len(half))
        for (dx, dy), p in zip(half, parts):
            if (dx, dy) == (0, 0):
                kept = p
            else:
                arrived.append(move(p, dx, dy, 0))

    hidden = lax.all_to_all(hidden, "feat", 0, 0)
    hidden = hidden.reshape(blocks, hid_local, LANES).transpose(1, 0, 2).reshape(hid_local, rows).T
    weight_part = grads[: peers * feat_local].reshape(peers, feat_local, hid)
    bias_part = jnp.broadcast_to(grads[peers * feat_local:], (peers, 8, hid))
    summed = jnp.sum(lax.all_to_all(jnp.concatenate([weight_part, bias_part], axis=1), "feat", 0, 0), axis=0)
    for i in range(4):
        pairs = []
        for n in range(slabs):
            x, y, c = n // 8, (n // 2) % 4, n % 2
            c, y, x = (c ^ 1, y, x) if i == 0 else (c, y ^ 1, x) if i == 1 else (c, 3 - y, x) if i == 2 else (c, y, x ^ 1)
            pairs.append((n, x * 8 + y * 2 + c))
        summed = summed + lax.ppermute(summed, "nodes", pairs)
    summed = summed * (rows * slabs) ** (-0.5)
    grad_weight = summed[:feat_local]
    grad_bias = lax.dynamic_slice(summed[feat_local], (place[0] * hid_local,), (hid_local,))

    grad_feats = pl.pallas_call(
        finish_kernel,
        out_shape=jax.ShapeDtypeStruct((feat_local, rows), F32),
        name="finish",
    )(kept, norm_blocks, *arrived).T
    return hidden, grad_weight, grad_bias, grad_feats


def solution(mesh):
    return jax.shard_map(
        on_device,
        mesh=mesh,
        in_specs=(
            P("nodes", "feat"),
            P("nodes", None, None, None, None),
            P("nodes", None, None),
            P("nodes", None, None),
            P("nodes", None),
            P("nodes"),
            P("feat", None),
            P("feat"),
            P("nodes", "feat"),
        ),
        out_specs=(P("nodes", "feat"), P("feat", None), P("feat"), P("nodes", "feat")),
        check_vma=False,
    )
```

```python
import functools

import jax
import jax.numpy as jnp
from jax import lax
from jax.experimental import pallas as pl
from jax.experimental.pallas import tpu as pltpu
from jax.sharding import PartitionSpec as P

LANES = 128
UNROLL = 8
BF16 = jnp.bfloat16
F32 = jnp.float32
META_COUNTS, META_ME = 16, 17


def spec(space):
    return pl.BlockSpec(memory_space=space)


ANY, VMEM, SMEM = pl.ANY, pltpu.VMEM, pltpu.SMEM


def params():
    return pltpu.CompilerParams(vmem_limit_bytes=16 << 20)


def scale_kernel(feats, norm, scaled):
    for b in range(scaled.shape[0]):
        scaled[b] = (norm[pl.ds(b, 1), :] * feats[:, pl.ds(b * LANES, LANES)].astype(F32)).astype(BF16)


def payload_kernel(cotangent, weight, bias, payload):
    peers, per_peer = payload.shape[0], payload.shape[1] - 2
    for b in range(peers * per_peer):
        payload[b // per_peer, b % per_peer] = cotangent[:, pl.ds(b * LANES, LANES)]
    w = jnp.concatenate([weight[:, :LANES], weight[:, LANES:]], axis=0)
    rest = jnp.concatenate([bias[...]] * (LANES // bias.shape[1]), axis=1)
    parts = []
    for _ in range(3):
        part = rest.astype(BF16).astype(F32)
        rest = rest - part
        parts.append(part)
    row = lax.broadcasted_iota(jnp.int32, (payload.shape[2], LANES), 0)
    packed = jnp.where(row == 0, parts[0], jnp.where(row == 1, parts[1], jnp.where(row == 2, parts[2], 0.0)))
    packed = packed.astype(BF16)
    for g in range(peers):
        payload[g, per_peer] = w
        payload[g, per_peer + 1] = packed


def slab_id(meta, hop):
    me = meta[META_ME, 0]
    dx, dy, dc = hop
    return ((((me >> 3) + dx) & 1) << 3) + ((((me >> 1) + dy) & 3) << 1) + ((me + dc) & 1)


def start_tiles(k, slab, count, tiles, buffer, sems):
    for chunk in range(tiles.shape[1] // UNROLL):
        @pl.when(chunk * UNROLL < count)
        def _():
            pltpu.make_async_copy(
                tiles.at[slab, pl.ds(chunk * UNROLL, UNROLL)],
                buffer.at[k, pl.ds(chunk * UNROLL, UNROLL)],
                sems.at[k, chunk],
            ).start()


def over_tiles(k, slab, count, meta, tiles, buffer, sems, source_of, target_of, dims, accumulator):
    def step(chunk, carry):
        first = chunk * UNROLL
        pltpu.make_async_copy(
            tiles.at[slab, pl.ds(first, UNROLL)], buffer.at[k, pl.ds(first, UNROLL)], sems.at[k, chunk]
        ).wait()
        products, targets = [], []
        for j in range(UNROLL):
            c = first + j
            entry = meta[slab, c]
            r = lax.dot_general(source_of(entry), buffer[k, c], (dims, ((), ())), preferred_element_type=F32)
            products.append(jnp.where(c < count, r, 0.0))
            targets.append(target_of(entry))
        for t, r in zip(targets, products):
            accumulator[t] = accumulator[t] + r
        return carry

    lax.fori_loop(0, (count + UNROLL - 1) // UNROLL, step, 0)


def cost(pieces, tiles):
    used = pieces * tiles.shape[1] // 2
    tile = tiles.shape[2]
    return pl.CostEstimate(
        flops=2 * used * 16 * tile * tile, transcendentals=0, bytes_accessed=used * tile * tile * 4
    )


def forward_kernel(hops, first, last, meta, *refs):
    refs = list(refs)
    pieces = len(hops)
    xs = [refs.pop(0) for _ in range(pieces)]
    tiles = refs.pop(0)
    start = None if first else refs.pop(0)
    norm = refs.pop(0) if last else None
    out, buffer, sems, x_buffer, x_sems, acc = refs
    loads = []
    for k in range(pieces):
        slab = slab_id(meta, hops[k])
        load = pltpu.make_async_copy(xs[k], x_buffer.at[k], x_sems.at[k])
        load.start()
        loads.append(load)
        if k == 0 and not first:
            seed = pltpu.make_async_copy(start, acc, x_sems.at[pieces])
            seed.start()
        start_tiles(k, slab, meta[META_COUNTS, slab], tiles, buffer, sems)
    if first:
        for b in range(acc.shape[0]):
            acc[b] = jnp.zeros(acc.shape[1:], F32)
    else:
        seed.wait()
    for k in range(pieces):
        slab = slab_id(meta, hops[k])
        loads[k].wait()
        over_tiles(
            k, slab, meta[META_COUNTS, slab], meta, tiles, buffer, sems,
            lambda entry, k=k: x_buffer[k, entry & 63], lambda entry: entry >> 6, ((1,), (1,)), acc,
        )
    if last:
        per_peer = out.shape[1]
        for b in range(acc.shape[0]):
            out[b // per_peer, b % per_peer] = (norm[pl.ds(b, 1), :] * acc[b]).astype(BF16)
    else:
        save = pltpu.make_async_copy(acc, out, x_sems.at[pieces + 1])
        save.start()
        save.wait()


def forward_call(hops, xs, meta, tiles, start, norm, peers):
    pieces = len(xs)
    first, last = start is None, norm is not None
    shape = xs[0].shape
    args = [meta, *xs, tiles]
    specs = [spec(SMEM)] + [spec(ANY)] * (pieces + 1)
    if not first:
        args.append(start)
        specs.append(spec(ANY))
    if last:
        args.append(norm)
        specs.append(spec(VMEM))
        out = jax.ShapeDtypeStruct((peers, shape[0] // peers, *shape[1:]), BF16)
    else:
        out = jax.ShapeDtypeStruct(shape, F32)
    return pl.pallas_call(
        functools.partial(forward_kernel, hops, first, last),
        out_shape=out, in_specs=specs, out_specs=spec(VMEM) if last else spec(ANY),
        scratch_shapes=[
            VMEM((pieces, *tiles.shape[1:]), BF16),
            pltpu.SemaphoreType.DMA((pieces, tiles.shape[1] // UNROLL)),
            VMEM((pieces, *shape), BF16),
            pltpu.SemaphoreType.DMA((pieces + 2,)),
            VMEM(shape, F32),
        ],
        compiler_params=params(), cost_estimate=cost(pieces, tiles), name="forward_tiles",
    )(*args)


def backward_kernel(hops, added, meta, *refs):
    refs = list(refs)
    pieces = len(hops)
    ys = refs.pop(0)
    tiles = refs.pop(0)
    adds = [refs.pop(0) for _ in range(pieces)] if added else None
    outs = [refs.pop(0) for _ in range(pieces)]
    buffer, sems, y_buffer, y_sem, acc, save_sems = refs[:6]
    if added:
        add_buffer, add_sems = refs[6:]
    load = pltpu.make_async_copy(ys, y_buffer, y_sem.at[0])
    load.start()
    seeds = []
    for k in range(pieces):
        slab = slab_id(meta, hops[k])
        start_tiles(k, slab, meta[META_COUNTS, slab], tiles, buffer, sems)
        if added:
            seed = pltpu.make_async_copy(adds[k], add_buffer.at[k], add_sems.at[k])
            seed.start()
            seeds.append(seed)
    per_peer = ys.shape[1]
    blocks = acc.shape[1]
    saves = []
    for k in range(pieces):
        slab = slab_id(meta, hops[k])
        if added:
            seeds[k].wait()
        for b in range(blocks):
            acc[k, b] = add_buffer[k, b].astype(F32) if added else jnp.zeros(acc.shape[2:], F32)
        if k == 0:
            load.wait()

        def source_of(entry):
            d = entry >> 6
            return y_buffer[d // per_peer, d % per_peer]

        over_tiles(
            k, slab, meta[META_COUNTS, slab], meta, tiles, buffer, sems, source_of,
            lambda entry: entry & 63, ((1,), (0,)), acc.at[k],
        )
        if outs[k].dtype == F32:
            save = pltpu.make_async_copy(acc.at[k], outs[k], save_sems.at[k])
        else:
            held = buffer.at[k, pl.ds(0, acc.shape[1] * acc.shape[2] // LANES)]
            rows = acc.shape[2]
            per_tile = LANES // rows
            for b in range(blocks):
                held[b // per_tile, pl.ds((b % per_tile) * rows, rows), :] = acc[k, b].astype(BF16)
            save = pltpu.make_async_copy(held, outs[k], save_sems.at[k])
        save.start()
        saves.append(save)
    for save in saves:
        save.wait()


def backward_call(hops, ys, meta, tiles, adds, kept):
    pieces = len(hops)
    rows = ys.shape[2]
    blocks = ys.shape[0] * ys.shape[1]
    added = adds is not None
    args = [meta, ys, tiles] + (list(adds) if added else [])
    specs = [spec(SMEM), spec(ANY), spec(ANY)] + [spec(ANY)] * (pieces if added else 0)
    packed = (blocks * rows // LANES, LANES, LANES)
    outs = [
        jax.ShapeDtypeStruct((blocks, rows, LANES), F32) if k == kept else jax.ShapeDtypeStruct(packed, BF16)
        for k in range(pieces)
    ]
    scratch = [
        VMEM((pieces, *tiles.shape[1:]), BF16),
        pltpu.SemaphoreType.DMA((pieces, tiles.shape[1] // UNROLL)),
        VMEM(ys.shape, BF16),
        pltpu.SemaphoreType.DMA((1,)),
        VMEM((pieces, blocks, rows, LANES), F32),
        pltpu.SemaphoreType.DMA((pieces,)),
    ]
    if added:
        scratch += [VMEM((pieces, blocks, rows, LANES), BF16), pltpu.SemaphoreType.DMA((pieces,))]
    parts = pl.pallas_call(
        functools.partial(backward_kernel, hops, added),
        out_shape=outs, in_specs=specs, out_specs=[spec(ANY)] * pieces, scratch_shapes=scratch,
        compiler_params=params(), cost_estimate=cost(pieces, tiles), name="backward_tiles",
    )(*args)
    return [p.reshape(blocks, rows, LANES) for p in parts]


def dense_kernel(place, agg, received, norm, back, sent):
    peers, blocks, feat_local = agg.shape[0], agg.shape[1], agg.shape[2]
    hid_local = sent.shape[2]
    halves = hid_local // feat_local
    weight = jnp.concatenate(
        [
            jnp.concatenate([received[g, blocks, pl.ds(h * feat_local, feat_local), :] for h in range(halves)], axis=1)
            for g in range(peers)
        ],
        axis=0,
    )
    bias_rows = []
    for g in range(peers):
        parts = received[g, blocks + 1].astype(F32)
        bias_rows.append((parts[0:1] + parts[1:2] + parts[2:3])[:, :hid_local])
    bias = jnp.concatenate(bias_rows, axis=1)
    bias = jnp.transpose(jnp.broadcast_to(bias, (8, bias.shape[1])))[:, 0:1]
    grad = jnp.zeros((peers * feat_local + 8, weight.shape[1]), F32)
    for b in range(blocks):
        agg_b = jnp.concatenate([agg[g, b] for g in range(peers)], axis=0)
        cot_b = jnp.concatenate([received[g, b] for g in range(peers)], axis=0).astype(F32)
        pre = lax.dot_general(weight, agg_b, (((0,), (0,)), ((), ())), preferred_element_type=F32) + bias
        sig = 1.0 / (1.0 + jnp.exp(-pre))
        hid = (pre * sig).astype(BF16)
        grad_pre = (cot_b * sig * (1.0 + pre * (1.0 - sig))).astype(BF16)
        back_b = jnp.dot(weight, grad_pre, preferred_element_type=F32)
        back_b = (norm[pl.ds(place[0] * blocks + b, 1), :] * back_b).astype(BF16)
        left = jnp.concatenate([agg_b, jnp.ones((8, LANES), BF16)], axis=0)
        grad = grad + lax.dot_general(left, grad_pre, (((1,), (1,)), ((), ())), preferred_element_type=F32)
        for g in range(peers):
            sent[g, b] = hid[g * hid_local:(g + 1) * hid_local]
            back[g, b] = back_b[g * feat_local:(g + 1) * feat_local]
    for g in range(peers):
        for source, slot in ((grad[g * feat_local:(g + 1) * feat_local], blocks), (grad[peers * feat_local:], blocks + 2)):
            high = source.astype(BF16).astype(F32)
            for i, part in enumerate((high, source - high)):
                part = jnp.concatenate([part[:, h * LANES:(h + 1) * LANES] for h in range(halves)], axis=0)
                short = hid_local - part.shape[0]
                if slot == blocks + 2:
                    sent[g, slot, pl.ds(i * part.shape[0], part.shape[0]), :] = part.astype(BF16)
                else:
                    sent[g, slot + i] = part.astype(BF16)


def collect_kernel(received, hidden, grads):
    peers, per_peer = received.shape[0], received.shape[1] - 3
    for b in range(peers * per_peer):
        hidden[:, pl.ds(b * LANES, LANES)] = received[b // per_peer, b % per_peer]
    rows = received.shape[2]
    total = jnp.zeros((rows, LANES), F32)
    tail = jnp.zeros((rows, LANES), F32)
    for g in range(peers):
        total = total + (received[g, per_peer].astype(F32) + received[g, per_peer + 1].astype(F32))
        tail = tail + received[g, per_peer + 2].astype(F32)
    grads[0:rows] = total
    grads[rows:2 * rows] = tail


def finish_kernel(kept, norm, *refs):
    out = refs[-1]
    for b in range(kept.shape[0]):
        total = kept[b]
        for r in refs[:-1]:
            total = total + r[b].astype(F32)
        out[:, pl.ds(b * LANES, LANES)] = norm[pl.ds(b, 1), :] * total


def on_device(feats, tiles, dst_block, src_block, tile_counts, norm, weight, bias, cotangent):
    rows, feat_local = feats.shape
    tile = tiles.shape[-1]
    blocks = rows // tile
    hid_local = cotangent.shape[1]
    peers = lax.axis_size("feat")
    slabs = lax.axis_size("nodes")
    per_peer = blocks // peers
    slots = tiles.shape[2]
    own_tiles = tiles[0]
    norm_blocks = norm.reshape(blocks, tile)
    me = lax.axis_index("nodes").astype(jnp.int32)
    place = lax.axis_index("feat").astype(jnp.int32).reshape(1)
    meta = jnp.concatenate(
        [
            src_block[0] + 64 * dst_block[0],
            jnp.concatenate([tile_counts, tile_counts], axis=1),
            jnp.full((1, slots), me, jnp.int32),
        ],
        axis=0,
    )

    def move(value, dx, dy, dc):
        pairs = []
        for i in range(slabs):
            x, y, c = i // 8, (i // 2) % 4, i % 2
            pairs.append((i, ((x + dx) % 2) * 8 + ((y + dy) % 4) * 2 + (c + dc) % 2))
        return lax.ppermute(value, "nodes", pairs)

    scaled = pl.pallas_call(
        scale_kernel,
        out_shape=jax.ShapeDtypeStruct((blocks, feat_local, LANES), BF16),
        compiler_params=params(), name="scale",
    )(feats.T, norm_blocks)
    payload = pl.pallas_call(
        payload_kernel,
        out_shape=jax.ShapeDtypeStruct((peers, per_peer + 2, hid_local, LANES), BF16),
        compiler_params=params(), name="payload",
    )(cotangent.T, weight, bias.reshape(1, hid_local))
    hops = [(0, 0), (0, 1), (0, 3), (1, 0), (1, 1), (1, 3), (0, 2), (1, 2)]
    pieces = {hop: scaled if hop == (0, 0) else move(scaled, *hop, 0) for hop in hops}
    received = lax.all_to_all(payload, "feat", 0, 0)
    total = None
    groups = [hops[:1], hops[1:4], hops[4:6], hops[6:]]
    for g, group in enumerate(groups):
        xs, froms = [], []
        for dx, dy in group:
            for dc in (0, 1):
                xs.append(move(pieces[dx, dy], 0, 0, 1) if dc else pieces[dx, dy])
                froms.append(((-dx) % 2, (-dy) % 4, dc))
        total = forward_call(froms, xs, meta, own_tiles, total, norm_blocks if g == len(groups) - 1 else None, peers)
    agg = lax.all_to_all(total, "feat", 0, 0)
    back, sent = pl.pallas_call(
        dense_kernel,
        out_shape=(
            jax.ShapeDtypeStruct((peers, per_peer, feat_local, LANES), BF16),
            jax.ShapeDtypeStruct((peers, per_peer + 3, hid_local, LANES), BF16),
        ),
        in_specs=[spec(SMEM), spec(VMEM), spec(VMEM), spec(VMEM)],
        compiler_params=params(), name="dense",
    )(place, agg, received, norm_blocks)
    back = lax.all_to_all(back, "feat", 0, 0)
    collected = lax.all_to_all(sent, "feat", 0, 0)

    order = [(1, 2), (0, 2), (1, 1), (1, 3), (0, 1), (0, 3), (1, 0), (0, 0)]
    halves = [order[:4], order[4:]]
    swapped = []
    for half in halves:
        parts = backward_call([(dx, dy, 1) for dx, dy in half], back, meta, own_tiles, None, None)
        swapped.append([move(p, 0, 0, 1) for p in parts])
    arrived, kept = [], None
    for half, adds in zip(halves, swapped):
        stay = half.index((0, 0)) if (0, 0) in half else None
        parts = backward_call([(dx, dy, 0) for dx, dy in half], back, meta, own_tiles, adds, stay)
        for (dx, dy), p in zip(half, parts):
            if (dx, dy) == (0, 0):
                kept = p
            else:
                arrived.append(move(p, dx, dy, 0))

    hidden, summed = pl.pallas_call(
        collect_kernel,
        out_shape=(
            jax.ShapeDtypeStruct((hid_local, rows), BF16),
            jax.ShapeDtypeStruct((2 * hid_local, LANES), F32),
        ),
        compiler_params=params(), name="collect",
    )(collected)
    for i in range(4):
        pairs = []
        for n in range(slabs):
            x, y, c = n // 8, (n // 2) % 4, n % 2
            c, y, x = (c ^ 1, y, x) if i == 0 else (c, y ^ 1, x) if i == 1 else (c, 3 - y, x) if i == 2 else (c, y, x ^ 1)
            pairs.append((n, x * 8 + y * 2 + c))
        summed = summed + lax.ppermute(summed, "nodes", pairs)
    summed = summed * (rows * slabs) ** (-0.5)
    halves_of = hid_local // feat_local
    grad_weight = jnp.concatenate([summed[h * feat_local:(h + 1) * feat_local] for h in range(halves_of)], axis=1)
    low = hid_local + 8 * halves_of
    bias_row = jnp.concatenate([summed[hid_local + 8 * h] + summed[low + 8 * h] for h in range(halves_of)])
    grad_bias = lax.dynamic_slice(bias_row, (place[0] * hid_local,), (hid_local,))

    grad_feats = pl.pallas_call(
        finish_kernel,
        out_shape=jax.ShapeDtypeStruct((feat_local, rows), F32),
        compiler_params=params(), name="finish",
    )(kept, norm_blocks, *arrived).T
    return hidden.T, grad_weight, grad_bias, grad_feats


def solution(mesh):
    return jax.shard_map(
        on_device,
        mesh=mesh,
        in_specs=(
            P("nodes", "feat"),
            P("nodes", None, None, None, None),
            P("nodes", None, None),
            P("nodes", None, None),
            P("nodes", None),
            P("nodes"),
            P("feat", None),
            P("feat"),
            P("nodes", "feat"),
        ),
        out_specs=(P("nodes", "feat"), P("feat", None), P("feat"), P("nodes", "feat")),
        check_vma=False,
    )
```

```python
import functools

import jax
import jax.numpy as jnp
from jax import lax
from jax.experimental import pallas as pl
from jax.experimental.pallas import tpu as pltpu
from jax.sharding import PartitionSpec as P

LANES = 128
UNROLL = 8
BF16 = jnp.bfloat16
F32 = jnp.float32
META_COUNTS, META_ME = 16, 17


def spec(space):
    return pl.BlockSpec(memory_space=space)


ANY, VMEM, SMEM, HBM = pl.ANY, pltpu.VMEM, pltpu.SMEM, pltpu.HBM


def params(megabytes=16):
    return pltpu.CompilerParams(vmem_limit_bytes=megabytes << 20)


def scale_kernel(feats, norm, scaled):
    for b in range(scaled.shape[0]):
        scaled[b] = (norm[pl.ds(b, 1), :] * feats[:, pl.ds(b * LANES, LANES)].astype(F32)).astype(BF16)


def payload_kernel(cotangent, weight, bias, payload):
    peers, per_peer = payload.shape[0], payload.shape[1] - 2
    for b in range(peers * per_peer):
        payload[b // per_peer, b % per_peer] = cotangent[:, pl.ds(b * LANES, LANES)]
    w = jnp.concatenate([weight[:, :LANES], weight[:, LANES:]], axis=0)
    rest = jnp.concatenate([bias[...]] * (LANES // bias.shape[1]), axis=1)
    parts = []
    for _ in range(3):
        part = rest.astype(BF16).astype(F32)
        rest = rest - part
        parts.append(part)
    row = lax.broadcasted_iota(jnp.int32, (payload.shape[2], LANES), 0)
    packed = jnp.where(row == 0, parts[0], jnp.where(row == 1, parts[1], jnp.where(row == 2, parts[2], 0.0)))
    packed = packed.astype(BF16)
    for g in range(peers):
        payload[g, per_peer] = w
        payload[g, per_peer + 1] = packed


def after(value, *held):
    return lax.optimization_barrier((value, *held))[0] if held else value


def slab_id(meta, hop):
    me = meta[META_ME, 0]
    dx, dy, dc = hop
    return ((((me >> 3) + dx) & 1) << 3) + ((((me >> 1) + dy) & 3) << 1) + ((me + dc) & 1)


def start_tiles(k, slab, count, tiles, buffer, sems):
    for chunk in range(tiles.shape[1] // UNROLL):
        @pl.when(chunk * UNROLL < count)
        def _():
            pltpu.make_async_copy(
                tiles.at[slab, pl.ds(chunk * UNROLL, UNROLL)],
                buffer.at[k, pl.ds(chunk * UNROLL, UNROLL)],
                sems.at[k, chunk],
            ).start()


def over_tiles(k, slab, count, meta, tiles, buffer, sems, source_of, target_of, dims, accumulator):
    def step(chunk, carry):
        first = chunk * UNROLL
        pltpu.make_async_copy(
            tiles.at[slab, pl.ds(first, UNROLL)], buffer.at[k, pl.ds(first, UNROLL)], sems.at[k, chunk]
        ).wait()
        products, targets = [], []
        for j in range(0, UNROLL, 2):
            c = first + j
            pair = [meta[slab, c], meta[slab, c + 1]]
            left = jnp.concatenate([source_of(e) for e in pair], axis=0)
            right = jnp.concatenate([buffer[k, c], buffer[k, c + 1]], axis=0 if dims[1] == (1,) else 1)
            r = lax.dot_general(left, right, (dims, ((), ())), preferred_element_type=F32)
            rows = r.shape[0] // 2
            for i in range(2):
                part = r[i * rows:(i + 1) * rows, i * LANES:(i + 1) * LANES]
                products.append(jnp.where(c + i < count, part, 0.0))
                targets.append(target_of(pair[i]))
        for t, r in zip(targets, products):
            accumulator[t] = accumulator[t] + r
        return carry

    lax.fori_loop(0, (count + UNROLL - 1) // UNROLL, step, 0)


def cost(pieces, tiles):
    used = pieces * tiles.shape[1] // 2
    tile = tiles.shape[2]
    return pl.CostEstimate(
        flops=2 * used * 16 * tile * tile, transcendentals=0, bytes_accessed=used * tile * tile * 4
    )


def forward_kernel(hops, where, first, last, meta, *refs):
    refs = list(refs)
    pieces = len(hops)
    arrays = [refs.pop(0) for _ in range(1 + max(a for a, _ in where))]
    xs = [arrays[a] if i is None else arrays[a].at[i] for a, i in where]
    tiles = refs.pop(0)
    start = None if first else refs.pop(0)
    norm = refs.pop(0) if last else None
    out, buffer, sems, x_buffer, x_sems, acc = refs
    loads = []
    for k in range(pieces):
        slab = slab_id(meta, hops[k])
        load = pltpu.make_async_copy(xs[k], x_buffer.at[k], x_sems.at[k])
        load.start()
        loads.append(load)
        if k == 0 and not first:
            seed = pltpu.make_async_copy(start, acc, x_sems.at[pieces])
            seed.start()
        start_tiles(k, slab, meta[META_COUNTS, slab], tiles, buffer, sems)
    if first:
        for b in range(acc.shape[0]):
            acc[b] = jnp.zeros(acc.shape[1:], F32)
    else:
        seed.wait()
    for k in range(pieces):
        slab = slab_id(meta, hops[k])
        loads[k].wait()
        over_tiles(
            k, slab, meta[META_COUNTS, slab], meta, tiles, buffer, sems,
            lambda entry, k=k: x_buffer[k, entry & 63], lambda entry: entry >> 6, ((1,), (1,)), acc,
        )
    if last:
        per_peer = out.shape[1]
        for b in range(acc.shape[0]):
            out[b // per_peer, b % per_peer] = (norm[pl.ds(b, 1), :] * acc[b]).astype(BF16)
    else:
        save = pltpu.make_async_copy(acc, out, x_sems.at[pieces + 1])
        save.start()
        save.wait()


def forward_call(entries, meta, tiles, start, norm, peers):
    pieces = len(entries)
    first, last = start is None, norm is not None
    arrays, where = [], []
    for array, index, _ in entries:
        at = [i for i, other in enumerate(arrays) if other is array]
        if not at:
            arrays.append(array)
        where.append((at[0] if at else len(arrays) - 1, index))
    hops = [hop for _, _, hop in entries]
    shape = arrays[0].shape if entries[0][1] is None else arrays[0].shape[1:]
    args = [meta, *arrays, tiles]
    specs = [spec(SMEM)] + [spec(ANY)] * len(arrays) + [spec(HBM)]
    if not first:
        args.append(start)
        specs.append(spec(ANY))
    if last:
        args.append(norm)
        specs.append(spec(VMEM))
        out = jax.ShapeDtypeStruct((peers, shape[0] // peers, *shape[1:]), BF16)
    else:
        out = jax.ShapeDtypeStruct(shape, F32)
    return pl.pallas_call(
        functools.partial(forward_kernel, hops, where, first, last),
        out_shape=out, in_specs=specs, out_specs=spec(VMEM) if last else spec(ANY),
        scratch_shapes=[
            VMEM((pieces, *tiles.shape[1:]), BF16),
            pltpu.SemaphoreType.DMA((pieces, tiles.shape[1] // UNROLL)),
            VMEM((pieces, *shape), BF16),
            pltpu.SemaphoreType.DMA((pieces + 2,)),
            VMEM(shape, F32),
        ],
        compiler_params=params(48), cost_estimate=cost(pieces, tiles), name="forward_tiles",
    )(*args)


def backward_kernel(hops, mode, meta, *refs):
    refs = list(refs)
    pieces = len(hops)
    added = mode != "swap"
    ys = refs.pop(0)
    tiles = refs.pop(0)
    adds = refs.pop(0) if added else None
    extra = refs.pop(0) if mode == "send" else None
    outs = [refs.pop(0) for _ in range(1 if mode == "swap" else pieces)]
    if mode == "swap":
        outs = [outs[0].at[k] for k in range(pieces)]
    buffer, sems, y_buffer, y_sem, acc, save_sems = refs[:6]
    if added:
        add_buffer, add_sems = refs[6:]
    load = pltpu.make_async_copy(ys, y_buffer, y_sem.at[0])
    load.start()
    seeds = []
    for k in range(pieces):
        slab = slab_id(meta, hops[k])
        start_tiles(k, slab, meta[META_COUNTS, slab], tiles, buffer, sems)
        if added:
            seed = pltpu.make_async_copy(adds.at[k], add_buffer.at[k], add_sems.at[k])
            seed.start()
            seeds.append(seed)
    blocks, rows = acc.shape[1], acc.shape[2]
    per_peer = blocks // ys.shape[0]
    per_tile = LANES // rows
    saves = []
    for k in range(pieces):
        slab = slab_id(meta, hops[k])
        if added:
            seeds[k].wait()
        for b in range(blocks):
            if added:
                acc[k, b] = add_buffer[k, b // per_tile, pl.ds((b % per_tile) * rows, rows), :].astype(F32)
            else:
                acc[k, b] = jnp.zeros(acc.shape[2:], F32)
        if k == 0:
            load.wait()

        def source_of(entry):
            d = entry >> 6
            return y_buffer[d // per_peer, d % per_peer]

        over_tiles(
            k, slab, meta[META_COUNTS, slab], meta, tiles, buffer, sems, source_of,
            lambda entry: entry & 63, ((1,), (0,)), acc.at[k],
        )
        if outs[k].dtype == F32:
            save = pltpu.make_async_copy(acc.at[k], outs[k], save_sems.at[k])
        else:
            held = buffer.at[k, pl.ds(0, outs[k].shape[0])]
            for b in range(blocks):
                held[b // per_tile, pl.ds((b % per_tile) * rows, rows), :] = acc[k, b].astype(BF16)
            if extra is not None:
                split(extra[...], held.at[blocks // per_tile])
            save = pltpu.make_async_copy(held, outs[k], save_sems.at[k])
        save.start()
        saves.append(save)
    for save in saves:
        save.wait()


def split(value, tile):
    high = value.astype(BF16)
    tile[0:value.shape[0], :] = high
    tile[value.shape[0]:2 * value.shape[0], :] = (value - high.astype(F32)).astype(BF16)


def joined(tile):
    half = tile.shape[0] // 2
    return tile[0:half, :].astype(F32) + tile[half:2 * half, :].astype(F32)


def backward_call(hops, mode, ys, blocks, meta, tiles, adds=None, extra=None):
    pieces = len(hops)
    rows = ys.shape[2]
    packed = (blocks * rows // LANES, LANES, LANES)
    more = (packed[0] + 1, LANES, LANES)
    args, specs = [meta, ys, tiles], [spec(SMEM), spec(ANY), spec(HBM)]
    if mode != "swap":
        args.append(adds)
        specs.append(spec(ANY))
    if mode == "swap":
        outs = jax.ShapeDtypeStruct((pieces, *packed), BF16)
    elif mode == "send":
        args.append(extra)
        specs.append(spec(VMEM))
        outs = [jax.ShapeDtypeStruct(more, BF16)] * pieces
    else:
        outs = [jax.ShapeDtypeStruct((blocks, rows, LANES), F32)] + [jax.ShapeDtypeStruct(packed, BF16)] * (pieces - 1)
    scratch = [
        VMEM((pieces, *tiles.shape[1:]), BF16),
        pltpu.SemaphoreType.DMA((pieces, tiles.shape[1] // UNROLL)),
        VMEM(ys.shape, BF16),
        pltpu.SemaphoreType.DMA((1,)),
        VMEM((pieces, blocks, rows, LANES), F32),
        pltpu.SemaphoreType.DMA((pieces,)),
    ]
    if mode != "swap":
        scratch += [VMEM((pieces, *packed), BF16), pltpu.SemaphoreType.DMA((pieces,))]
    return pl.pallas_call(
        functools.partial(backward_kernel, hops, mode),
        out_shape=outs, in_specs=specs,
        out_specs=spec(ANY) if mode == "swap" else [spec(ANY)] * pieces, scratch_shapes=scratch,
        compiler_params=params(48), cost_estimate=cost(pieces, tiles), name="backward_tiles",
    )(*args)


def dense_kernel(place, agg, received, norm, back, sent):
    peers, blocks, feat_local = agg.shape[0], agg.shape[1], agg.shape[2]
    hid_local = sent.shape[2]
    halves = hid_local // feat_local
    weight = jnp.concatenate(
        [
            jnp.concatenate([received[g, blocks, pl.ds(h * feat_local, feat_local), :] for h in range(halves)], axis=1)
            for g in range(peers)
        ],
        axis=0,
    )
    bias_rows = []
    for g in range(peers):
        parts = received[g, blocks + 1].astype(F32)
        bias_rows.append((parts[0:1] + parts[1:2] + parts[2:3])[:, :hid_local])
    bias = jnp.concatenate(bias_rows, axis=1)
    bias = jnp.transpose(jnp.broadcast_to(bias, (8, bias.shape[1])))[:, 0:1]
    grad = jnp.zeros((peers * feat_local + 8, weight.shape[1]), F32)
    for b in range(blocks):
        agg_b = jnp.concatenate([agg[g, b] for g in range(peers)], axis=0)
        cot_b = jnp.concatenate([received[g, b] for g in range(peers)], axis=0).astype(F32)
        pre = lax.dot_general(weight, agg_b, (((0,), (0,)), ((), ())), preferred_element_type=F32) + bias
        sig = 1.0 / (1.0 + jnp.exp(-pre))
        hid = (pre * sig).astype(BF16)
        grad_pre = (cot_b * sig * (1.0 + pre * (1.0 - sig))).astype(BF16)
        back_b = jnp.dot(weight, grad_pre, preferred_element_type=F32)
        back_b = (norm[pl.ds(place[0] * blocks + b, 1), :] * back_b).astype(BF16)
        left = jnp.concatenate([agg_b, jnp.ones((8, LANES), BF16)], axis=0)
        grad = grad + lax.dot_general(left, grad_pre, (((1,), (1,)), ((), ())), preferred_element_type=F32)
        for g in range(peers):
            sent[g, b] = hid[g * hid_local:(g + 1) * hid_local]
            back[g, b] = back_b[g * feat_local:(g + 1) * feat_local]
    for g in range(peers):
        for source, slot in ((grad[g * feat_local:(g + 1) * feat_local], blocks), (grad[peers * feat_local:], blocks + 4)):
            high = source.astype(BF16).astype(F32)
            for i, part in enumerate((high, source - high)):
                part = jnp.concatenate([part[:, h * LANES:(h + 1) * LANES] for h in range(halves)], axis=0)
                part = part.astype(BF16)
                if slot == blocks + 4:
                    back[g, slot + i] = part
                else:
                    for h in range(halves):
                        back[g, slot + i * halves + h] = part[h * feat_local:(h + 1) * feat_local]


def collect_kernel(received, hidden):
    peers, per_peer = received.shape[0], received.shape[1]
    for b in range(peers * per_peer):
        hidden[:, pl.ds(b * LANES, LANES)] = received[b // per_peer, b % per_peer]


def weight_sums_kernel(back, sums):
    rows = back.shape[2]
    first = back.shape[1] - 6
    for i in range(2):
        total = jnp.zeros((rows, LANES), F32)
        for g in range(back.shape[0]):
            total = total + (back[g, first + i].astype(F32) + back[g, first + 2 + i].astype(F32))
        sums[i * rows:(i + 1) * rows] = total
        tail = jnp.zeros((rows, LANES), F32)
        for g in range(back.shape[0]):
            tail = tail + back[g, first + 4 + i].astype(F32)
        sums[(2 + i) * rows:(3 + i) * rows] = tail


def cross_kernel(own, down, up, far, out):
    last = out.shape[0] - 1
    for t in range(last):
        total = (own[t].astype(F32) + far[t].astype(F32)) + (down[t].astype(F32) + up[t].astype(F32))
        out[t] = total.astype(BF16)
    split((joined(own.at[last]) + joined(far.at[last])) + (joined(down.at[last]) + joined(up.at[last])), out.at[last])


def finish_with_scale(scale, place, kept, norm, down, up, far, sent, came, out, grad_weight, grad_bias):
    rows = kept.shape[1]
    per_tile = LANES // rows
    for b in range(kept.shape[0]):
        total = kept[b]
        for r in (down, up, far, came):
            total = total + r[b // per_tile, pl.ds((b % per_tile) * rows, rows), :].astype(F32)
        out[:, pl.ds(b * LANES, LANES)] = norm[pl.ds(b, 1), :] * total
    last = sent.shape[0] - 1
    sums = (joined(sent.at[last]) + joined(came.at[last])) * scale
    hid_local = grad_bias.shape[1]
    halves = grad_weight.shape[1] // LANES
    for h in range(halves):
        grad_weight[:, h * LANES:(h + 1) * LANES] = sums[h * rows:(h + 1) * rows]
    low = 2 * rows + 8 * halves
    bias = jnp.zeros((1, hid_local), F32)
    for h in range(halves):
        row = sums[2 * rows + 8 * h:2 * rows + 8 * h + 1] + sums[low + 8 * h:low + 8 * h + 1]
        for i in range(LANES // hid_local):
            here = place[0] == h * (LANES // hid_local) + i
            bias = jnp.where(here, row[:, i * hid_local:(i + 1) * hid_local], bias)
    grad_bias[...] = bias


def on_device(feats, tiles, dst_block, src_block, tile_counts, norm, weight, bias, cotangent):
    rows, feat_local = feats.shape
    tile = tiles.shape[-1]
    blocks = rows // tile
    hid_local = cotangent.shape[1]
    peers = lax.axis_size("feat")
    slabs = lax.axis_size("nodes")
    per_peer = blocks // peers
    slots = tiles.shape[2]
    own_tiles = tiles[0]
    norm_blocks = norm.reshape(blocks, tile)
    me = lax.axis_index("nodes").astype(jnp.int32)
    place = lax.axis_index("feat").astype(jnp.int32).reshape(1)
    meta = jnp.concatenate(
        [
            src_block[0] + 64 * dst_block[0],
            jnp.concatenate([tile_counts, tile_counts], axis=1),
            jnp.full((1, slots), me, jnp.int32),
        ],
        axis=0,
    )

    def move(value, dx, dy, dc):
        pairs = []
        for i in range(slabs):
            x, y, c = i // 8, (i // 2) % 4, i % 2
            pairs.append((i, ((x + dx) % 2) * 8 + ((y + dy) % 4) * 2 + (c + dc) % 2))
        return lax.ppermute(value, "nodes", pairs)

    scaled = pl.pallas_call(
        scale_kernel,
        out_shape=jax.ShapeDtypeStruct((blocks, feat_local, LANES), BF16),
        compiler_params=params(), name="scale",
    )(feats.T, norm_blocks)
    payload = pl.pallas_call(
        payload_kernel,
        out_shape=jax.ShapeDtypeStruct((peers, per_peer + 2, hid_local, LANES), BF16),
        compiler_params=params(), name="payload",
    )(cotangent.T, weight, bias.reshape(1, hid_local))
    across = move(scaled, 1, 0, 0)
    down, up = move(scaled, 0, 1, 0), move(scaled, 0, 3, 0)
    entries = [(scaled, None, (0, 0, 0)), (move(scaled, 0, 0, 1), None, (0, 0, 1))]
    across, down, up = lax.optimization_barrier((across, down, up))
    down_across, up_across = move(across, 0, 1, 0), move(across, 0, 3, 0)
    received = lax.all_to_all(payload, "feat", 0, 0)
    far, far_across, received = lax.optimization_barrier((scaled, across, received))
    far, far_across = move(far, 0, 2, 0), move(far_across, 0, 2, 0)

    def group(values, hops):
        moved = move(jnp.stack(values), 0, 0, 1)
        near = [(v, None, (*hop, 0)) for v, hop in zip(values, hops)]
        return near, [(moved, i, (*hop, 1)) for i, hop in enumerate(hops)]

    near, other = group([across, down, up], [(1, 0), (0, 3), (0, 1)])
    total = forward_call(entries + near + other, meta, own_tiles, None, None, peers)
    *values, total = lax.optimization_barrier((down_across, up_across, far, far_across, total))
    near, other = group(values, [(1, 3), (1, 1), (0, 2), (1, 2)])
    total = forward_call(near, meta, own_tiles, total, None, peers)
    total = forward_call(other, meta, own_tiles, total, norm_blocks, peers)
    agg = lax.all_to_all(total, "feat", 0, 0)
    back, sent = pl.pallas_call(
        dense_kernel,
        out_shape=(
            jax.ShapeDtypeStruct((peers, per_peer + 6, feat_local, LANES), BF16),
            jax.ShapeDtypeStruct((peers, per_peer, hid_local, LANES), BF16),
        ),
        in_specs=[spec(SMEM), spec(VMEM), spec(VMEM), spec(VMEM)],
        compiler_params=params(), name="dense",
    )(place, agg, received, norm_blocks)
    back = lax.all_to_all(back, "feat", 0, 0)

    summed = pl.pallas_call(
        weight_sums_kernel,
        out_shape=jax.ShapeDtypeStruct((4 * feat_local, LANES), F32),
        compiler_params=params(), name="weight_sums",
    )(back)
    ways = [(0, 0), (0, 1), (0, 3), (0, 2)]
    over = [(1, dy) for _, dy in ways]
    mine = backward_call([(*hop, 1) for hop in over], "swap", back, blocks, meta, own_tiles)
    mine_too = backward_call([(*hop, 1) for hop in ways], "swap", after(back, mine), blocks, meta, own_tiles)
    swapped, mine_too, theirs = lax.optimization_barrier((move(mine, 0, 0, 1), mine_too, move(summed, 0, 0, 1)))
    sums = backward_call([(*hop, 0) for hop in over], "send", back, blocks, meta, own_tiles, swapped, summed + theirs)
    crossing = [move(p, *hop, 0) for p, hop in zip(sums[1:], ways[1:])]
    swapped = after(move(mine_too, 0, 0, 1), sums[1])
    parts = backward_call([(*hop, 0) for hop in ways], "keep", back, blocks, meta, own_tiles, swapped)
    arrived = [move(p, *hop, 0) for p, hop in zip(parts[1:], ways[1:])]
    *crossing, _ = lax.optimization_barrier((*crossing, parts[1]))
    crossed = pl.pallas_call(
        cross_kernel,
        out_shape=jax.ShapeDtypeStruct(sums[0].shape, BF16),
        compiler_params=params(), name="cross",
    )(sums[0], *crossing)
    hidden = pl.pallas_call(
        collect_kernel,
        out_shape=jax.ShapeDtypeStruct((hid_local, rows), BF16),
        compiler_params=params(), name="collect",
    )(lax.all_to_all(after(sent, parts[1]), "feat", 0, 0))
    came = move(crossed, 1, 0, 0)
    grad_feats, grad_weight, grad_bias = pl.pallas_call(
        functools.partial(finish_with_scale, float((rows * slabs) ** -0.5)),
        out_shape=(
            jax.ShapeDtypeStruct((feat_local, rows), F32),
            jax.ShapeDtypeStruct(weight.shape, F32),
            jax.ShapeDtypeStruct((1, hid_local), F32),
        ),
        in_specs=[spec(SMEM)] + [spec(VMEM)] * 7,
        compiler_params=params(), name="finish",
    )(place, parts[0], norm_blocks, *arrived, crossed, came)
    return hidden.T, grad_weight, grad_bias.reshape(hid_local), grad_feats.T


def solution(mesh):
    return jax.shard_map(
        on_device,
        mesh=mesh,
        in_specs=(
            P("nodes", "feat"),
            P("nodes", None, None, None, None),
            P("nodes", None, None),
            P("nodes", None, None),
            P("nodes", None),
            P("nodes"),
            P("feat", None),
            P("feat"),
            P("nodes", "feat"),
        ),
        out_specs=(P("nodes", "feat"), P("feat", None), P("feat"), P("nodes", "feat")),
        check_vma=False,
    )
```

```python
import functools

import jax
import jax.numpy as jnp
from jax import lax
from jax.experimental import pallas as pl
from jax.experimental.pallas import tpu as pltpu
from jax.sharding import PartitionSpec as P

LANES = 128
UNROLL, LOAD = 16, 8
BF16 = jnp.bfloat16
F32 = jnp.float32
META_COUNTS, META_ME = 16, 17


def spec(space):
    return pl.BlockSpec(memory_space=space)


ANY, VMEM, SMEM, HBM = pl.ANY, pltpu.VMEM, pltpu.SMEM, pltpu.HBM


def params(megabytes=16):
    return pltpu.CompilerParams(vmem_limit_bytes=megabytes << 20)


def scale_kernel(feats, norm, scaled):
    for b in range(scaled.shape[0]):
        scaled[b] = (norm[pl.ds(b, 1), :] * feats[:, pl.ds(b * LANES, LANES)].astype(F32)).astype(BF16)


def payload_kernel(cotangent, weight, bias, payload):
    peers, per_peer = payload.shape[0], payload.shape[1] - 2
    for b in range(peers * per_peer):
        payload[b // per_peer, b % per_peer] = cotangent[:, pl.ds(b * LANES, LANES)]
    w = jnp.concatenate([weight[:, :LANES], weight[:, LANES:]], axis=0)
    rest = jnp.concatenate([bias[...]] * (LANES // bias.shape[1]), axis=1)
    parts = []
    for _ in range(3):
        part = rest.astype(BF16).astype(F32)
        rest = rest - part
        parts.append(part)
    row = lax.broadcasted_iota(jnp.int32, (payload.shape[2], LANES), 0)
    packed = jnp.where(row == 0, parts[0], jnp.where(row == 1, parts[1], jnp.where(row == 2, parts[2], 0.0)))
    packed = packed.astype(BF16)
    for g in range(peers):
        payload[g, per_peer] = w
        payload[g, per_peer + 1] = packed


def after(value, *held):
    return lax.optimization_barrier((value, *held))[0] if held else value


def slab_id(meta, hop):
    me = meta[META_ME, 0]
    dx, dy, dc = hop
    return ((((me >> 3) + dx) & 1) << 3) + ((((me >> 1) + dy) & 3) << 1) + ((me + dc) & 1)


def start_tiles(k, slab, count, tiles, buffer, sems):
    for chunk in range(tiles.shape[1] // LOAD):
        @pl.when(chunk * LOAD < count)
        def _():
            load_tiles(k, slab, chunk, tiles, buffer, sems).start()


def load_tiles(k, slab, chunk, tiles, buffer, sems):
    these = pl.ds(chunk * LOAD, LOAD)
    return pltpu.make_async_copy(tiles.at[slab, these], buffer.at[k, these], sems.at[k, chunk])


def over_tiles(k, slab, count, meta, tiles, buffer, sems, source_of, target_of, dims, accumulator):
    def step(chunk, carry):
        first = chunk * UNROLL
        for part in range(UNROLL // LOAD):
            @pl.when(first + part * LOAD < count)
            def _():
                load_tiles(k, slab, chunk * (UNROLL // LOAD) + part, tiles, buffer, sems).wait()
        products, targets = [], []
        for j in range(0, UNROLL, 2):
            c = first + j
            pair = [meta[slab, c], meta[slab, c + 1]]
            left = jnp.concatenate([source_of(e) for e in pair], axis=0)
            right = jnp.concatenate([buffer[k, c], buffer[k, c + 1]], axis=0 if dims[1] == (1,) else 1)
            r = lax.dot_general(left, right, (dims, ((), ())), preferred_element_type=F32)
            rows = r.shape[0] // 2
            for i in range(2):
                part = r[i * rows:(i + 1) * rows, i * LANES:(i + 1) * LANES]
                products.append(jnp.where(c + i < count, part, 0.0))
                targets.append(target_of(pair[i]))
        for t, r in zip(targets, products):
            accumulator[t] = accumulator[t] + r
        return carry

    lax.fori_loop(0, (count + UNROLL - 1) // UNROLL, step, 0)


def cost(pieces, tiles):
    used = pieces * tiles.shape[1] // 2
    tile = tiles.shape[2]
    return pl.CostEstimate(
        flops=2 * used * 16 * tile * tile, transcendentals=0, bytes_accessed=used * tile * tile * 4
    )


def forward_kernel(hops, where, first, last, meta, *refs):
    refs = list(refs)
    pieces = len(hops)
    arrays = [refs.pop(0) for _ in range(1 + max(a for a, _ in where))]
    xs = [arrays[a] if i is None else arrays[a].at[i] for a, i in where]
    tiles = refs.pop(0)
    start = None if first else refs.pop(0)
    norm = refs.pop(0) if last else None
    out, buffer, sems, x_buffer, x_sems, acc = refs
    loads = []
    for k in range(pieces):
        slab = slab_id(meta, hops[k])
        load = pltpu.make_async_copy(xs[k], x_buffer.at[k], x_sems.at[k])
        load.start()
        loads.append(load)
        if k == 0 and not first:
            seed = pltpu.make_async_copy(start, acc, x_sems.at[pieces])
            seed.start()
        start_tiles(k, slab, meta[META_COUNTS, slab], tiles, buffer, sems)
    if first:
        for b in range(acc.shape[0]):
            acc[b] = jnp.zeros(acc.shape[1:], F32)
    else:
        seed.wait()
    for k in range(pieces):
        slab = slab_id(meta, hops[k])
        loads[k].wait()
        over_tiles(
            k, slab, meta[META_COUNTS, slab], meta, tiles, buffer, sems,
            lambda entry, k=k: x_buffer[k, entry & 63], lambda entry: entry >> 6, ((1,), (1,)), acc,
        )
    if last:
        per_peer = out.shape[1]
        for b in range(acc.shape[0]):
            out[b // per_peer, b % per_peer] = (norm[pl.ds(b, 1), :] * acc[b]).astype(BF16)
    else:
        save = pltpu.make_async_copy(acc, out, x_sems.at[pieces + 1])
        save.start()
        save.wait()


def forward_call(entries, meta, tiles, start, norm, peers):
    pieces = len(entries)
    first, last = start is None, norm is not None
    arrays, where = [], []
    for array, index, _ in entries:
        at = [i for i, other in enumerate(arrays) if other is array]
        if not at:
            arrays.append(array)
        where.append((at[0] if at else len(arrays) - 1, index))
    hops = [hop for _, _, hop in entries]
    shape = arrays[0].shape if entries[0][1] is None else arrays[0].shape[1:]
    args = [meta, *arrays, tiles]
    specs = [spec(SMEM)] + [spec(ANY)] * len(arrays) + [spec(HBM)]
    if not first:
        args.append(start)
        specs.append(spec(ANY))
    if last:
        args.append(norm)
        specs.append(spec(VMEM))
        out = jax.ShapeDtypeStruct((peers, shape[0] // peers, *shape[1:]), BF16)
    else:
        out = jax.ShapeDtypeStruct(shape, F32)
    return pl.pallas_call(
        functools.partial(forward_kernel, hops, where, first, last),
        out_shape=out, in_specs=specs, out_specs=spec(VMEM) if last else spec(ANY),
        scratch_shapes=[
            VMEM((pieces, *tiles.shape[1:]), BF16),
            pltpu.SemaphoreType.DMA((pieces, tiles.shape[1] // LOAD)),
            VMEM((pieces, *shape), BF16),
            pltpu.SemaphoreType.DMA((pieces + 2,)),
            VMEM(shape, F32),
        ],
        compiler_params=params(48), cost_estimate=cost(pieces, tiles), name="forward_tiles",
    )(*args)


def backward_kernel(hops, mode, meta, *refs):
    refs = list(refs)
    pieces = len(hops)
    added = mode != "swap"
    ys = refs.pop(0)
    tiles = refs.pop(0)
    adds = refs.pop(0) if added else None
    extra = refs.pop(0) if mode == "send" else None
    outs = [refs.pop(0) for _ in range(1 if mode == "swap" else pieces)]
    if mode == "swap":
        outs = [outs[0].at[k] for k in range(pieces)]
    buffer, sems, y_buffer, y_sem, acc, save_sems = refs[:6]
    if added:
        add_buffer, add_sems = refs[6:]
    load = pltpu.make_async_copy(ys, y_buffer, y_sem.at[0])
    load.start()
    seeds = []
    for k in range(pieces):
        slab = slab_id(meta, hops[k])
        start_tiles(k, slab, meta[META_COUNTS, slab], tiles, buffer, sems)
        if added:
            seed = pltpu.make_async_copy(adds.at[k], add_buffer.at[k], add_sems.at[k])
            seed.start()
            seeds.append(seed)
    blocks, rows = acc.shape[1], acc.shape[2]
    per_peer = blocks // ys.shape[0]
    per_tile = LANES // rows
    saves = []
    for k in range(pieces):
        slab = slab_id(meta, hops[k])
        if added:
            seeds[k].wait()
        for b in range(blocks):
            if added:
                acc[k, b] = add_buffer[k, b // per_tile, pl.ds((b % per_tile) * rows, rows), :].astype(F32)
            else:
                acc[k, b] = jnp.zeros(acc.shape[2:], F32)
        if k == 0:
            load.wait()

        def source_of(entry):
            d = entry >> 6
            return y_buffer[d // per_peer, d % per_peer]

        over_tiles(
            k, slab, meta[META_COUNTS, slab], meta, tiles, buffer, sems, source_of,
            lambda entry: entry & 63, ((1,), (0,)), acc.at[k],
        )
        if outs[k].dtype == F32:
            save = pltpu.make_async_copy(acc.at[k], outs[k], save_sems.at[k])
        else:
            held = buffer.at[k, pl.ds(0, outs[k].shape[0])]
            for b in range(blocks):
                held[b // per_tile, pl.ds((b % per_tile) * rows, rows), :] = acc[k, b].astype(BF16)
            if extra is not None:
                split(extra[...], held.at[blocks // per_tile])
            save = pltpu.make_async_copy(held, outs[k], save_sems.at[k])
        save.start()
        saves.append(save)
    for save in saves:
        save.wait()


def split(value, tile):
    high = value.astype(BF16)
    tile[0:value.shape[0], :] = high
    tile[value.shape[0]:2 * value.shape[0], :] = (value - high.astype(F32)).astype(BF16)


def joined(tile):
    half = tile.shape[0] // 2
    return tile[0:half, :].astype(F32) + tile[half:2 * half, :].astype(F32)


def backward_call(hops, mode, ys, blocks, meta, tiles, adds=None, extra=None):
    pieces = len(hops)
    rows = ys.shape[2]
    packed = (blocks * rows // LANES, LANES, LANES)
    more = (packed[0] + 1, LANES, LANES)
    args, specs = [meta, ys, tiles], [spec(SMEM), spec(ANY), spec(HBM)]
    if mode != "swap":
        args.append(adds)
        specs.append(spec(ANY))
    if mode == "swap":
        outs = jax.ShapeDtypeStruct((pieces, *packed), BF16)
    elif mode == "send":
        args.append(extra)
        specs.append(spec(VMEM))
        outs = [jax.ShapeDtypeStruct(more, BF16)] * pieces
    else:
        outs = [jax.ShapeDtypeStruct((blocks, rows, LANES), F32)] + [jax.ShapeDtypeStruct(packed, BF16)] * (pieces - 1)
    scratch = [
        VMEM((pieces, *tiles.shape[1:]), BF16),
        pltpu.SemaphoreType.DMA((pieces, tiles.shape[1] // LOAD)),
        VMEM(ys.shape, BF16),
        pltpu.SemaphoreType.DMA((1,)),
        VMEM((pieces, blocks, rows, LANES), F32),
        pltpu.SemaphoreType.DMA((pieces,)),
    ]
    if mode != "swap":
        scratch += [VMEM((pieces, *packed), BF16), pltpu.SemaphoreType.DMA((pieces,))]
    return pl.pallas_call(
        functools.partial(backward_kernel, hops, mode),
        out_shape=outs, in_specs=specs,
        out_specs=spec(ANY) if mode == "swap" else [spec(ANY)] * pieces, scratch_shapes=scratch,
        compiler_params=params(48), cost_estimate=cost(pieces, tiles), name="backward_tiles",
    )(*args)


def dense_kernel(place, agg, received, norm, back, sent):
    peers, blocks, feat_local = agg.shape[0], agg.shape[1], agg.shape[2]
    hid_local = sent.shape[2]
    halves = hid_local // feat_local
    weight = jnp.concatenate(
        [
            jnp.concatenate([received[g, blocks, pl.ds(h * feat_local, feat_local), :] for h in range(halves)], axis=1)
            for g in range(peers)
        ],
        axis=0,
    )
    bias_rows = []
    for g in range(peers):
        parts = received[g, blocks + 1].astype(F32)
        bias_rows.append((parts[0:1] + parts[1:2] + parts[2:3])[:, :hid_local])
    bias = jnp.concatenate(bias_rows, axis=1)
    bias = jnp.transpose(jnp.broadcast_to(bias, (8, bias.shape[1])))[:, 0:1]
    grad = jnp.zeros((peers * feat_local + 8, weight.shape[1]), F32)
    for b in range(blocks):
        agg_b = jnp.concatenate([agg[g, b] for g in range(peers)], axis=0)
        cot_b = jnp.concatenate([received[g, b] for g in range(peers)], axis=0).astype(F32)
        pre = lax.dot_general(weight, agg_b, (((0,), (0,)), ((), ())), preferred_element_type=F32) + bias
        sig = 1.0 / (1.0 + jnp.exp(-pre))
        hid = (pre * sig).astype(BF16)
        grad_pre = (cot_b * sig * (1.0 + pre * (1.0 - sig))).astype(BF16)
        back_b = jnp.dot(weight, grad_pre, preferred_element_type=F32)
        back_b = (norm[pl.ds(place[0] * blocks + b, 1), :] * back_b).astype(BF16)
        left = jnp.concatenate([agg_b, jnp.ones((8, LANES), BF16)], axis=0)
        grad = grad + lax.dot_general(left, grad_pre, (((1,), (1,)), ((), ())), preferred_element_type=F32)
        for g in range(peers):
            sent[g, b] = hid[g * hid_local:(g + 1) * hid_local]
            back[g, b] = back_b[g * feat_local:(g + 1) * feat_local]
    for g in range(peers):
        for source, slot in ((grad[g * feat_local:(g + 1) * feat_local], blocks), (grad[peers * feat_local:], blocks + 4)):
            high = source.astype(BF16).astype(F32)
            for i, part in enumerate((high, source - high)):
                part = jnp.concatenate([part[:, h * LANES:(h + 1) * LANES] for h in range(halves)], axis=0)
                part = part.astype(BF16)
                if slot == blocks + 4:
                    back[g, slot + i] = part
                else:
                    for h in range(halves):
                        back[g, slot + i * halves + h] = part[h * feat_local:(h + 1) * feat_local]


def collect_kernel(received, hidden):
    peers, per_peer = received.shape[0], received.shape[1]
    for b in range(peers * per_peer):
        hidden[:, pl.ds(b * LANES, LANES)] = received[b // per_peer, b % per_peer]


def weight_sums_kernel(back, sums):
    rows = back.shape[2]
    first = back.shape[1] - 6
    for i in range(2):
        total = jnp.zeros((rows, LANES), F32)
        for g in range(back.shape[0]):
            total = total + (back[g, first + i].astype(F32) + back[g, first + 2 + i].astype(F32))
        sums[i * rows:(i + 1) * rows] = total
        tail = jnp.zeros((rows, LANES), F32)
        for g in range(back.shape[0]):
            tail = tail + back[g, first + 4 + i].astype(F32)
        sums[(2 + i) * rows:(3 + i) * rows] = tail


def cross_kernel(own, down, up, far, out):
    last = out.shape[0] - 1
    for t in range(last):
        total = (own[t].astype(F32) + far[t].astype(F32)) + (down[t].astype(F32) + up[t].astype(F32))
        out[t] = total.astype(BF16)
    split((joined(own.at[last]) + joined(far.at[last])) + (joined(down.at[last]) + joined(up.at[last])), out.at[last])


def finish_with_scale(scale, place, kept, norm, down, up, far, sent, came, out, grad_weight, grad_bias):
    rows = kept.shape[1]
    per_tile = LANES // rows
    for b in range(kept.shape[0]):
        total = kept[b]
        for r in (down, up, far, came):
            total = total + r[b // per_tile, pl.ds((b % per_tile) * rows, rows), :].astype(F32)
        out[:, pl.ds(b * LANES, LANES)] = norm[pl.ds(b, 1), :] * total
    last = sent.shape[0] - 1
    sums = (joined(sent.at[last]) + joined(came.at[last])) * scale
    hid_local = grad_bias.shape[1]
    halves = grad_weight.shape[1] // LANES
    for h in range(halves):
        grad_weight[:, h * LANES:(h + 1) * LANES] = sums[h * rows:(h + 1) * rows]
    low = 2 * rows + 8 * halves
    bias = jnp.zeros((1, hid_local), F32)
    for h in range(halves):
        row = sums[2 * rows + 8 * h:2 * rows + 8 * h + 1] + sums[low + 8 * h:low + 8 * h + 1]
        for i in range(LANES // hid_local):
            here = place[0] == h * (LANES // hid_local) + i
            bias = jnp.where(here, row[:, i * hid_local:(i + 1) * hid_local], bias)
    grad_bias[...] = bias


def on_device(feats, tiles, dst_block, src_block, tile_counts, norm, weight, bias, cotangent):
    rows, feat_local = feats.shape
    tile = tiles.shape[-1]
    blocks = rows // tile
    hid_local = cotangent.shape[1]
    peers = lax.axis_size("feat")
    slabs = lax.axis_size("nodes")
    per_peer = blocks // peers
    slots = tiles.shape[2]
    own_tiles = tiles[0]
    norm_blocks = norm.reshape(blocks, tile)
    me = lax.axis_index("nodes").astype(jnp.int32)
    place = lax.axis_index("feat").astype(jnp.int32).reshape(1)
    meta = jnp.concatenate(
        [
            src_block[0] + 64 * dst_block[0],
            jnp.concatenate([tile_counts, tile_counts], axis=1),
            jnp.full((1, slots), me, jnp.int32),
        ],
        axis=0,
    )

    def move(value, dx, dy, dc):
        pairs = []
        for i in range(slabs):
            x, y, c = i // 8, (i // 2) % 4, i % 2
            pairs.append((i, ((x + dx) % 2) * 8 + ((y + dy) % 4) * 2 + (c + dc) % 2))
        return lax.ppermute(value, "nodes", pairs)

    scaled = pl.pallas_call(
        scale_kernel,
        out_shape=jax.ShapeDtypeStruct((blocks, feat_local, LANES), BF16),
        compiler_params=params(56), name="scale",
    )(feats.T, norm_blocks)
    payload = pl.pallas_call(
        payload_kernel,
        out_shape=jax.ShapeDtypeStruct((peers, per_peer + 2, hid_local, LANES), BF16),
        compiler_params=params(56), name="payload",
    )(cotangent.T, weight, bias.reshape(1, hid_local))
    across = move(scaled, 1, 0, 0)
    down, up = move(scaled, 0, 1, 0), move(scaled, 0, 3, 0)
    entries = [(scaled, None, (0, 0, 0)), (move(scaled, 0, 0, 1), None, (0, 0, 1))]
    across, down, up = lax.optimization_barrier((across, down, up))
    down_across, up_across = move(across, 0, 1, 0), move(across, 0, 3, 0)
    received = lax.all_to_all(payload, "feat", 0, 0)
    far, far_across, received = lax.optimization_barrier((scaled, across, received))
    far, far_across = move(far, 0, 2, 0), move(far_across, 0, 2, 0)

    def group(values, hops):
        moved = move(jnp.stack(values), 0, 0, 1)
        near = [(v, None, (*hop, 0)) for v, hop in zip(values, hops)]
        return near, [(moved, i, (*hop, 1)) for i, hop in enumerate(hops)]

    near, other = group([across, down, up], [(1, 0), (0, 3), (0, 1)])
    total = forward_call(entries + near + other, meta, own_tiles, None, None, peers)
    *values, total = lax.optimization_barrier((down_across, up_across, far, far_across, total))
    near, other = group(values, [(1, 3), (1, 1), (0, 2), (1, 2)])
    total = forward_call(near, meta, own_tiles, total, None, peers)
    total = forward_call(other, meta, own_tiles, total, norm_blocks, peers)
    agg = lax.all_to_all(total, "feat", 0, 0)
    back, sent = pl.pallas_call(
        dense_kernel,
        out_shape=(
            jax.ShapeDtypeStruct((peers, per_peer + 6, feat_local, LANES), BF16),
            jax.ShapeDtypeStruct((peers, per_peer, hid_local, LANES), BF16),
        ),
        in_specs=[spec(SMEM), spec(VMEM), spec(VMEM), spec(VMEM)],
        compiler_params=params(), name="dense",
    )(place, agg, received, norm_blocks)
    back = lax.all_to_all(back, "feat", 0, 0)

    summed = pl.pallas_call(
        weight_sums_kernel,
        out_shape=jax.ShapeDtypeStruct((4 * feat_local, LANES), F32),
        compiler_params=params(), name="weight_sums",
    )(back)
    ways = [(0, 0), (0, 1), (0, 3), (0, 2)]
    over = [(1, dy) for _, dy in ways]
    mine = backward_call([(*hop, 1) for hop in over], "swap", back, blocks, meta, own_tiles)
    mine_too = backward_call([(*hop, 1) for hop in ways], "swap", after(back, mine), blocks, meta, own_tiles)
    swapped, mine_too, theirs = lax.optimization_barrier((move(mine, 0, 0, 1), mine_too, move(summed, 0, 0, 1)))
    sums = backward_call([(*hop, 0) for hop in over], "send", back, blocks, meta, own_tiles, swapped, summed + theirs)
    crossing = [move(p, *hop, 0) for p, hop in zip(sums[1:], ways[1:])]
    swapped = after(move(mine_too, 0, 0, 1), sums[1])
    parts = backward_call([(*hop, 0) for hop in ways], "keep", back, blocks, meta, own_tiles, swapped)
    arrived = [move(p, *hop, 0) for p, hop in zip(parts[1:], ways[1:])]
    *crossing, _ = lax.optimization_barrier((*crossing, parts[1]))
    crossed = pl.pallas_call(
        cross_kernel,
        out_shape=jax.ShapeDtypeStruct(sums[0].shape, BF16),
        compiler_params=params(), name="cross",
    )(sums[0], *crossing)
    hidden = pl.pallas_call(
        collect_kernel,
        out_shape=jax.ShapeDtypeStruct((hid_local, rows), BF16),
        compiler_params=params(), name="collect",
    )(lax.all_to_all(after(sent, parts[1]), "feat", 0, 0))
    came = move(crossed, 1, 0, 0)
    grad_feats, grad_weight, grad_bias = pl.pallas_call(
        functools.partial(finish_with_scale, float((rows * slabs) ** -0.5)),
        out_shape=(
            jax.ShapeDtypeStruct((feat_local, rows), F32),
            jax.ShapeDtypeStruct(weight.shape, F32),
            jax.ShapeDtypeStruct((1, hid_local), F32),
        ),
        in_specs=[spec(SMEM)] + [spec(VMEM)] * 7,
        compiler_params=params(), name="finish",
    )(after(place, hidden), parts[0], norm_blocks, *arrived, crossed, came)
    return hidden.T, grad_weight, grad_bias.reshape(hid_local), grad_feats.T


def solution(mesh):
    return jax.shard_map(
        on_device,
        mesh=mesh,
        in_specs=(
            P("nodes", "feat"),
            P("nodes", None, None, None, None),
            P("nodes", None, None),
            P("nodes", None, None),
            P("nodes", None),
            P("nodes"),
            P("feat", None),
            P("feat"),
            P("nodes", "feat"),
        ),
        out_specs=(P("nodes", "feat"), P("feat", None), P("feat"), P("nodes", "feat")),
        check_vma=False,
    )
```

```python
import functools

import jax
import jax.numpy as jnp
from jax import lax
from jax.experimental import pallas as pl
from jax.experimental.pallas import tpu as pltpu
from jax.sharding import PartitionSpec as P

LANES = 128
UNROLL, LOAD = 16, 16
BF16 = jnp.bfloat16
F32 = jnp.float32
META_COUNTS, META_ME = 16, 17


def spec(space):
    return pl.BlockSpec(memory_space=space)


ANY, VMEM, SMEM, HBM = pl.ANY, pltpu.VMEM, pltpu.SMEM, pltpu.HBM


def params(megabytes=16):
    return pltpu.CompilerParams(vmem_limit_bytes=megabytes << 20)


def scale_kernel(feats, norm, scaled):
    for b in range(scaled.shape[0]):
        scaled[b] = (norm[pl.ds(b, 1), :] * feats[:, pl.ds(b * LANES, LANES)].astype(F32)).astype(BF16)


def payload_kernel(cotangent, weight, bias, payload):
    peers, per_peer = payload.shape[0], payload.shape[1] - 2
    for b in range(peers * per_peer):
        payload[b // per_peer, b % per_peer] = cotangent[:, pl.ds(b * LANES, LANES)]
    w = jnp.concatenate([weight[:, :LANES], weight[:, LANES:]], axis=0)
    rest = jnp.concatenate([bias[...]] * (LANES // bias.shape[1]), axis=1)
    parts = []
    for _ in range(3):
        part = rest.astype(BF16).astype(F32)
        rest = rest - part
        parts.append(part)
    row = lax.broadcasted_iota(jnp.int32, (payload.shape[2], LANES), 0)
    packed = jnp.where(row == 0, parts[0], jnp.where(row == 1, parts[1], jnp.where(row == 2, parts[2], 0.0)))
    packed = packed.astype(BF16)
    for g in range(peers):
        payload[g, per_peer] = w
        payload[g, per_peer + 1] = packed


def after(value, *held):
    return lax.optimization_barrier((value, *held))[0] if held else value


def slab_id(meta, hop):
    me = meta[META_ME, 0]
    dx, dy, dc = hop
    return ((((me >> 3) + dx) & 1) << 3) + ((((me >> 1) + dy) & 3) << 1) + ((me + dc) & 1)


def start_tiles(k, slab, count, tiles, buffer, sems):
    for chunk in range(tiles.shape[1] // LOAD):
        @pl.when(chunk * LOAD < count)
        def _():
            load_tiles(k, slab, chunk, tiles, buffer, sems).start()


def load_tiles(k, slab, chunk, tiles, buffer, sems):
    these = pl.ds(chunk * LOAD, LOAD)
    return pltpu.make_async_copy(tiles.at[slab, these], buffer.at[k, these], sems.at[k, chunk])


def over_tiles(k, slab, count, meta, tiles, buffer, sems, source_of, target_of, dims, accumulator):
    def step(chunk, carry):
        first = chunk * UNROLL
        for part in range(UNROLL // LOAD):
            @pl.when(first + part * LOAD < count)
            def _():
                load_tiles(k, slab, chunk * (UNROLL // LOAD) + part, tiles, buffer, sems).wait()
        products, targets = [], []
        for j in range(0, UNROLL, 2):
            c = first + j
            pair = [meta[slab, c], meta[slab, c + 1]]
            left = jnp.concatenate([source_of(e) for e in pair], axis=0)
            right = jnp.concatenate([buffer[k, c], buffer[k, c + 1]], axis=0 if dims[1] == (1,) else 1)
            r = lax.dot_general(left, right, (dims, ((), ())), preferred_element_type=F32)
            rows = r.shape[0] // 2
            for i in range(2):
                part = r[i * rows:(i + 1) * rows, i * LANES:(i + 1) * LANES]
                products.append(jnp.where(c + i < count, part, 0.0))
                targets.append(target_of(pair[i]))
        for t, r in zip(targets, products):
            accumulator[t] = accumulator[t] + r
        return carry

    lax.fori_loop(0, (count + UNROLL - 1) // UNROLL, step, 0)


def cost(pieces, tiles):
    used = pieces * tiles.shape[1] // 2
    tile = tiles.shape[2]
    return pl.CostEstimate(
        flops=2 * used * 16 * tile * tile, transcendentals=0, bytes_accessed=used * tile * tile * 4
    )


def forward_kernel(hops, where, first, last, meta, *refs):
    refs = list(refs)
    pieces = len(hops)
    arrays = [refs.pop(0) for _ in range(1 + max(a for a, _ in where))]
    xs = [arrays[a] if i is None else arrays[a].at[i] for a, i in where]
    tiles = refs.pop(0)
    start = None if first else refs.pop(0)
    norm = refs.pop(0) if last else None
    out, buffer, sems, x_buffer, x_sems, acc = refs
    loads = []
    for k in range(pieces):
        slab = slab_id(meta, hops[k])
        load = pltpu.make_async_copy(xs[k], x_buffer.at[k], x_sems.at[k])
        load.start()
        loads.append(load)
        if k == 0 and not first:
            seed = pltpu.make_async_copy(start, acc, x_sems.at[pieces])
            seed.start()
        start_tiles(k, slab, meta[META_COUNTS, slab], tiles, buffer, sems)
    if first:
        for b in range(acc.shape[0]):
            acc[b] = jnp.zeros(acc.shape[1:], F32)
    else:
        seed.wait()
    for k in range(pieces):
        slab = slab_id(meta, hops[k])
        loads[k].wait()
        over_tiles(
            k, slab, meta[META_COUNTS, slab], meta, tiles, buffer, sems,
            lambda entry, k=k: x_buffer[k, entry & 63], lambda entry: entry >> 6, ((1,), (1,)), acc,
        )
    if last:
        per_peer = out.shape[1]
        for b in range(acc.shape[0]):
            out[b // per_peer, b % per_peer] = (norm[pl.ds(b, 1), :] * acc[b]).astype(BF16)
    else:
        save = pltpu.make_async_copy(acc, out, x_sems.at[pieces + 1])
        save.start()
        save.wait()


def forward_call(entries, meta, tiles, start, norm, peers):
    pieces = len(entries)
    first, last = start is None, norm is not None
    arrays, where = [], []
    for array, index, _ in entries:
        at = [i for i, other in enumerate(arrays) if other is array]
        if not at:
            arrays.append(array)
        where.append((at[0] if at else len(arrays) - 1, index))
    hops = [hop for _, _, hop in entries]
    shape = arrays[0].shape if entries[0][1] is None else arrays[0].shape[1:]
    args = [meta, *arrays, tiles]
    specs = [spec(SMEM)] + [spec(ANY)] * len(arrays) + [spec(HBM)]
    if not first:
        args.append(start)
        specs.append(spec(ANY))
    if last:
        args.append(norm)
        specs.append(spec(VMEM))
        out = jax.ShapeDtypeStruct((peers, shape[0] // peers, *shape[1:]), BF16)
    else:
        out = jax.ShapeDtypeStruct(shape, F32)
    return pl.pallas_call(
        functools.partial(forward_kernel, hops, where, first, last),
        out_shape=out, in_specs=specs, out_specs=spec(VMEM) if last else spec(ANY),
        scratch_shapes=[
            VMEM((pieces, *tiles.shape[1:]), BF16),
            pltpu.SemaphoreType.DMA((pieces, tiles.shape[1] // LOAD)),
            VMEM((pieces, *shape), BF16),
            pltpu.SemaphoreType.DMA((pieces + 2,)),
            VMEM(shape, F32),
        ],
        compiler_params=params(48), cost_estimate=cost(pieces, tiles), name="forward_tiles",
    )(*args)


def backward_kernel(hops, mode, meta, *refs):
    refs = list(refs)
    pieces = len(hops)
    added = mode != "swap"
    ys = refs.pop(0)
    tiles = refs.pop(0)
    adds = refs.pop(0) if added else None
    extra = refs.pop(0) if mode == "send" else None
    outs = [refs.pop(0) for _ in range(1 if mode == "swap" else pieces)]
    if mode == "swap":
        outs = [outs[0].at[k] for k in range(pieces)]
    buffer, sems, y_buffer, y_sem, acc, save_sems = refs[:6]
    if added:
        add_buffer, add_sems = refs[6:]
    load = pltpu.make_async_copy(ys, y_buffer, y_sem.at[0])
    load.start()
    seeds = []
    for k in range(pieces):
        slab = slab_id(meta, hops[k])
        start_tiles(k, slab, meta[META_COUNTS, slab], tiles, buffer, sems)
        if added:
            seed = pltpu.make_async_copy(adds.at[k], add_buffer.at[k], add_sems.at[k])
            seed.start()
            seeds.append(seed)
    blocks, rows = acc.shape[1], acc.shape[2]
    per_peer = blocks // ys.shape[0]
    per_tile = LANES // rows
    saves = []
    for k in range(pieces):
        slab = slab_id(meta, hops[k])
        if added:
            seeds[k].wait()
        for b in range(blocks):
            if added:
                acc[k, b] = add_buffer[k, b // per_tile, pl.ds((b % per_tile) * rows, rows), :].astype(F32)
            else:
                acc[k, b] = jnp.zeros(acc.shape[2:], F32)
        if k == 0:
            load.wait()

        def source_of(entry):
            d = entry >> 6
            return y_buffer[d // per_peer, d % per_peer]

        over_tiles(
            k, slab, meta[META_COUNTS, slab], meta, tiles, buffer, sems, source_of,
            lambda entry: entry & 63, ((1,), (0,)), acc.at[k],
        )
        if outs[k].dtype == F32:
            save = pltpu.make_async_copy(acc.at[k], outs[k], save_sems.at[k])
        else:
            held = buffer.at[k, pl.ds(0, outs[k].shape[0])]
            for b in range(blocks):
                held[b // per_tile, pl.ds((b % per_tile) * rows, rows), :] = acc[k, b].astype(BF16)
            if extra is not None:
                split(extra[...], held.at[blocks // per_tile])
            save = pltpu.make_async_copy(held, outs[k], save_sems.at[k])
        save.start()
        saves.append(save)
    for save in saves:
        save.wait()


def split(value, tile):
    high = value.astype(BF16)
    tile[0:value.shape[0], :] = high
    tile[value.shape[0]:2 * value.shape[0], :] = (value - high.astype(F32)).astype(BF16)


def joined(tile):
    half = tile.shape[0] // 2
    return tile[0:half, :].astype(F32) + tile[half:2 * half, :].astype(F32)


def backward_call(hops, mode, ys, blocks, meta, tiles, adds=None, extra=None):
    pieces = len(hops)
    rows = ys.shape[2]
    packed = (blocks * rows // LANES, LANES, LANES)
    more = (packed[0] + 1, LANES, LANES)
    args, specs = [meta, ys, tiles], [spec(SMEM), spec(ANY), spec(HBM)]
    if mode != "swap":
        args.append(adds)
        specs.append(spec(ANY))
    if mode == "swap":
        outs = jax.ShapeDtypeStruct((pieces, *packed), BF16)
    elif mode == "send":
        args.append(extra)
        specs.append(spec(VMEM))
        outs = [jax.ShapeDtypeStruct(more, BF16)] * pieces
    else:
        outs = [jax.ShapeDtypeStruct((blocks, rows, LANES), F32)] + [jax.ShapeDtypeStruct(packed, BF16)] * (pieces - 1)
    scratch = [
        VMEM((pieces, *tiles.shape[1:]), BF16),
        pltpu.SemaphoreType.DMA((pieces, tiles.shape[1] // LOAD)),
        VMEM(ys.shape, BF16),
        pltpu.SemaphoreType.DMA((1,)),
        VMEM((pieces, blocks, rows, LANES), F32),
        pltpu.SemaphoreType.DMA((pieces,)),
    ]
    if mode != "swap":
        scratch += [VMEM((pieces, *packed), BF16), pltpu.SemaphoreType.DMA((pieces,))]
    return pl.pallas_call(
        functools.partial(backward_kernel, hops, mode),
        out_shape=outs, in_specs=specs,
        out_specs=spec(ANY) if mode == "swap" else [spec(ANY)] * pieces, scratch_shapes=scratch,
        compiler_params=params(48), cost_estimate=cost(pieces, tiles), name="backward_tiles",
    )(*args)


def dense_kernel(place, agg, received, norm, back, sent):
    peers, blocks, feat_local = agg.shape[0], agg.shape[1], agg.shape[2]
    hid_local = sent.shape[2]
    halves = hid_local // feat_local
    weight = jnp.concatenate(
        [
            jnp.concatenate([received[g, blocks, pl.ds(h * feat_local, feat_local), :] for h in range(halves)], axis=1)
            for g in range(peers)
        ],
        axis=0,
    )
    bias_rows = []
    for g in range(peers):
        parts = received[g, blocks + 1].astype(F32)
        bias_rows.append((parts[0:1] + parts[1:2] + parts[2:3])[:, :hid_local])
    bias = jnp.concatenate(bias_rows, axis=1)
    bias = jnp.transpose(jnp.broadcast_to(bias, (8, bias.shape[1])))[:, 0:1]
    grad = jnp.zeros((peers * feat_local + 8, weight.shape[1]), F32)
    for b in range(blocks):
        agg_b = jnp.concatenate([agg[g, b] for g in range(peers)], axis=0)
        cot_b = jnp.concatenate([received[g, b] for g in range(peers)], axis=0).astype(F32)
        pre = lax.dot_general(weight, agg_b, (((0,), (0,)), ((), ())), preferred_element_type=F32) + bias
        sig = 1.0 / (1.0 + jnp.exp(-pre))
        hid = (pre * sig).astype(BF16)
        grad_pre = (cot_b * sig * (1.0 + pre * (1.0 - sig))).astype(BF16)
        back_b = jnp.dot(weight, grad_pre, preferred_element_type=F32)
        back_b = (norm[pl.ds(place[0] * blocks + b, 1), :] * back_b).astype(BF16)
        left = jnp.concatenate([agg_b, jnp.ones((8, LANES), BF16)], axis=0)
        grad = grad + lax.dot_general(left, grad_pre, (((1,), (1,)), ((), ())), preferred_element_type=F32)
        for g in range(peers):
            sent[g, b] = hid[g * hid_local:(g + 1) * hid_local]
            back[g, b] = back_b[g * feat_local:(g + 1) * feat_local]
    for g in range(peers):
        for source, slot in ((grad[g * feat_local:(g + 1) * feat_local], blocks), (grad[peers * feat_local:], blocks + 4)):
            high = source.astype(BF16).astype(F32)
            for i, part in enumerate((high, source - high)):
                part = jnp.concatenate([part[:, h * LANES:(h + 1) * LANES] for h in range(halves)], axis=0)
                part = part.astype(BF16)
                if slot == blocks + 4:
                    back[g, slot + i] = part
                else:
                    for h in range(halves):
                        back[g, slot + i * halves + h] = part[h * feat_local:(h + 1) * feat_local]


def collect_kernel(received, hidden):
    peers, per_peer = received.shape[0], received.shape[1]
    for b in range(peers * per_peer):
        hidden[:, pl.ds(b * LANES, LANES)] = received[b // per_peer, b % per_peer]


def weight_sums_kernel(back, sums):
    rows = back.shape[2]
    first = back.shape[1] - 6
    for i in range(2):
        total = jnp.zeros((rows, LANES), F32)
        for g in range(back.shape[0]):
            total = total + (back[g, first + i].astype(F32) + back[g, first + 2 + i].astype(F32))
        sums[i * rows:(i + 1) * rows] = total
        tail = jnp.zeros((rows, LANES), F32)
        for g in range(back.shape[0]):
            tail = tail + back[g, first + 4 + i].astype(F32)
        sums[(2 + i) * rows:(3 + i) * rows] = tail


def cross_kernel(own, down, up, far, out):
    last = out.shape[0] - 1
    for t in range(last):
        total = (own[t].astype(F32) + far[t].astype(F32)) + (down[t].astype(F32) + up[t].astype(F32))
        out[t] = total.astype(BF16)
    split((joined(own.at[last]) + joined(far.at[last])) + (joined(down.at[last]) + joined(up.at[last])), out.at[last])


def finish_with_scale(scale, place, kept, norm, down, up, far, sent, came, out, grad_weight, grad_bias):
    rows = kept.shape[1]
    per_tile = LANES // rows
    for b in range(kept.shape[0]):
        total = kept[b]
        for r in (down, up, far, came):
            total = total + r[b // per_tile, pl.ds((b % per_tile) * rows, rows), :].astype(F32)
        out[:, pl.ds(b * LANES, LANES)] = norm[pl.ds(b, 1), :] * total
    last = sent.shape[0] - 1
    sums = (joined(sent.at[last]) + joined(came.at[last])) * scale
    hid_local = grad_bias.shape[1]
    halves = grad_weight.shape[1] // LANES
    for h in range(halves):
        grad_weight[:, h * LANES:(h + 1) * LANES] = sums[h * rows:(h + 1) * rows]
    low = 2 * rows + 8 * halves
    bias = jnp.zeros((1, hid_local), F32)
    for h in range(halves):
        row = sums[2 * rows + 8 * h:2 * rows + 8 * h + 1] + sums[low + 8 * h:low + 8 * h + 1]
        for i in range(LANES // hid_local):
            here = place[0] == h * (LANES // hid_local) + i
            bias = jnp.where(here, row[:, i * hid_local:(i + 1) * hid_local], bias)
    grad_bias[...] = bias


def on_device(feats, tiles, dst_block, src_block, tile_counts, norm, weight, bias, cotangent):
    rows, feat_local = feats.shape
    tile = tiles.shape[-1]
    blocks = rows // tile
    hid_local = cotangent.shape[1]
    peers = lax.axis_size("feat")
    slabs = lax.axis_size("nodes")
    per_peer = blocks // peers
    slots = tiles.shape[2]
    own_tiles = tiles[0]
    norm_blocks = norm.reshape(blocks, tile)
    me = lax.axis_index("nodes").astype(jnp.int32)
    place = lax.axis_index("feat").astype(jnp.int32).reshape(1)
    meta = jnp.concatenate(
        [
            src_block[0] + 64 * dst_block[0],
            jnp.concatenate([tile_counts, tile_counts], axis=1),
            jnp.full((1, slots), me, jnp.int32),
        ],
        axis=0,
    )

    def move(value, dx, dy, dc):
        pairs = []
        for i in range(slabs):
            x, y, c = i // 8, (i // 2) % 4, i % 2
            pairs.append((i, ((x + dx) % 2) * 8 + ((y + dy) % 4) * 2 + (c + dc) % 2))
        return lax.ppermute(value, "nodes", pairs)

    scaled = pl.pallas_call(
        scale_kernel,
        out_shape=jax.ShapeDtypeStruct((blocks, feat_local, LANES), BF16),
        compiler_params=params(56), name="scale",
    )(feats.T, norm_blocks)
    payload = pl.pallas_call(
        payload_kernel,
        out_shape=jax.ShapeDtypeStruct((peers, per_peer + 2, hid_local, LANES), BF16),
        compiler_params=params(56), name="payload",
    )(cotangent.T, weight, bias.reshape(1, hid_local))
    across = move(scaled, 1, 0, 0)
    down, up = move(scaled, 0, 1, 0), move(scaled, 0, 3, 0)
    entries = [(scaled, None, (0, 0, 0)), (move(scaled, 0, 0, 1), None, (0, 0, 1))]
    across, down, up = lax.optimization_barrier((across, down, up))
    down_across, up_across = move(across, 0, 1, 0), move(across, 0, 3, 0)
    received = lax.all_to_all(payload, "feat", 0, 0)
    far, far_across, received = lax.optimization_barrier((scaled, across, received))
    far, far_across = move(far, 0, 2, 0), move(far_across, 0, 2, 0)

    def group(values, hops):
        moved = move(jnp.stack(values), 0, 0, 1)
        near = [(v, None, (*hop, 0)) for v, hop in zip(values, hops)]
        return near, [(moved, i, (*hop, 1)) for i, hop in enumerate(hops)]

    near, other = group([across, down, up], [(1, 0), (0, 3), (0, 1)])
    total = forward_call(entries + near + other, meta, own_tiles, None, None, peers)
    *values, total = lax.optimization_barrier((down_across, up_across, far, far_across, total))
    near, other = group(values, [(1, 3), (1, 1), (0, 2), (1, 2)])
    total = forward_call(near, meta, own_tiles, total, None, peers)
    total = forward_call(other, meta, own_tiles, total, norm_blocks, peers)
    agg = lax.all_to_all(total, "feat", 0, 0)
    back, sent = pl.pallas_call(
        dense_kernel,
        out_shape=(
            jax.ShapeDtypeStruct((peers, per_peer + 6, feat_local, LANES), BF16),
            jax.ShapeDtypeStruct((peers, per_peer, hid_local, LANES), BF16),
        ),
        in_specs=[spec(SMEM), spec(VMEM), spec(VMEM), spec(VMEM)],
        compiler_params=params(), name="dense",
    )(place, agg, received, norm_blocks)
    back = lax.all_to_all(back, "feat", 0, 0)

    summed = pl.pallas_call(
        weight_sums_kernel,
        out_shape=jax.ShapeDtypeStruct((4 * feat_local, LANES), F32),
        compiler_params=params(), name="weight_sums",
    )(back)
    ways = [(0, 0), (0, 1), (0, 3), (0, 2)]
    over = [(1, dy) for _, dy in ways]
    mine = backward_call([(*hop, 1) for hop in over], "swap", back, blocks, meta, own_tiles)
    mine_too = backward_call([(*hop, 1) for hop in ways], "swap", after(back, mine), blocks, meta, own_tiles)
    swapped, mine_too, theirs = lax.optimization_barrier((move(mine, 0, 0, 1), mine_too, move(summed, 0, 0, 1)))
    sums = backward_call([(*hop, 0) for hop in over], "send", back, blocks, meta, own_tiles, swapped, summed + theirs)
    crossing = [move(p, *hop, 0) for p, hop in zip(sums[1:], ways[1:])]
    swapped = after(move(mine_too, 0, 0, 1), sums[1])
    parts = backward_call([(*hop, 0) for hop in ways], "keep", back, blocks, meta, own_tiles, swapped)
    arrived = [move(p, *hop, 0) for p, hop in zip(parts[1:], ways[1:])]
    *crossing, arrived[2] = lax.optimization_barrier((*crossing, arrived[2]))
    crossed = pl.pallas_call(
        cross_kernel,
        out_shape=jax.ShapeDtypeStruct(sums[0].shape, BF16),
        compiler_params=params(), name="cross",
    )(sums[0], *crossing)
    hidden = pl.pallas_call(
        collect_kernel,
        out_shape=jax.ShapeDtypeStruct((hid_local, rows), BF16),
        compiler_params=params(), name="collect",
    )(lax.all_to_all(after(sent, parts[1]), "feat", 0, 0))
    came = move(crossed, 1, 0, 0)
    grad_feats, grad_weight, grad_bias = pl.pallas_call(
        functools.partial(finish_with_scale, float((rows * slabs) ** -0.5)),
        out_shape=(
            jax.ShapeDtypeStruct((feat_local, rows), F32),
            jax.ShapeDtypeStruct(weight.shape, F32),
            jax.ShapeDtypeStruct((1, hid_local), F32),
        ),
        in_specs=[spec(SMEM)] + [spec(VMEM)] * 7,
        compiler_params=params(), name="finish",
    )(after(place, hidden), parts[0], norm_blocks, *arrived, crossed, came)
    return hidden.T, grad_weight, grad_bias.reshape(hid_local), grad_feats.T


def solution(mesh):
    return jax.shard_map(
        on_device,
        mesh=mesh,
        in_specs=(
            P("nodes", "feat"),
            P("nodes", None, None, None, None),
            P("nodes", None, None),
            P("nodes", None, None),
            P("nodes", None),
            P("nodes"),
            P("feat", None),
            P("feat"),
            P("nodes", "feat"),
        ),
        out_specs=(P("nodes", "feat"), P("feat", None), P("feat"), P("nodes", "feat")),
        check_vma=False,
    )
```

```python
import functools

import jax
import jax.numpy as jnp
from jax import lax
from jax.experimental import pallas as pl
from jax.experimental.pallas import tpu as pltpu
from jax.sharding import PartitionSpec as P

LANES = 128
UNROLL, LOAD = 16, 16
BF16 = jnp.bfloat16
F32 = jnp.float32
META_COUNTS, META_ME = 16, 17


def spec(space):
    return pl.BlockSpec(memory_space=space)


ANY, VMEM, SMEM, HBM = pl.ANY, pltpu.VMEM, pltpu.SMEM, pltpu.HBM


def params(megabytes=16):
    return pltpu.CompilerParams(vmem_limit_bytes=megabytes << 20)


def scale_kernel(feats, norm, scaled):
    for b in range(scaled.shape[0]):
        scaled[b] = (norm[pl.ds(b, 1), :] * feats[:, pl.ds(b * LANES, LANES)].astype(F32)).astype(BF16)


def payload_kernel(cotangent, weight, bias, payload):
    peers, per_peer = payload.shape[0], payload.shape[1] - 2
    for b in range(peers * per_peer):
        payload[b // per_peer, b % per_peer] = cotangent[:, pl.ds(b * LANES, LANES)]
    w = jnp.concatenate([weight[:, :LANES], weight[:, LANES:]], axis=0)
    rest = jnp.concatenate([bias[...]] * (LANES // bias.shape[1]), axis=1)
    parts = []
    for _ in range(3):
        part = rest.astype(BF16).astype(F32)
        rest = rest - part
        parts.append(part)
    row = lax.broadcasted_iota(jnp.int32, (payload.shape[2], LANES), 0)
    packed = jnp.where(row == 0, parts[0], jnp.where(row == 1, parts[1], jnp.where(row == 2, parts[2], 0.0)))
    packed = packed.astype(BF16)
    for g in range(peers):
        payload[g, per_peer] = w
        payload[g, per_peer + 1] = packed


def after(value, *held):
    return lax.optimization_barrier((value, *held))[0] if held else value


def slab_id(meta, hop):
    me = meta[META_ME, 0]
    dx, dy, dc = hop
    return ((((me >> 3) + dx) & 1) << 3) + ((((me >> 1) + dy) & 3) << 1) + ((me + dc) & 1)


def start_tiles(k, slab, count, tiles, buffer, sems):
    for chunk in range(tiles.shape[1] // LOAD):
        @pl.when(chunk * LOAD < count)
        def _():
            load_tiles(k, slab, chunk, tiles, buffer, sems).start()


def load_tiles(k, slab, chunk, tiles, buffer, sems):
    these = pl.ds(chunk * LOAD, LOAD)
    return pltpu.make_async_copy(tiles.at[slab, these], buffer.at[k, these], sems.at[k, chunk])


def over_tiles(k, slab, count, meta, tiles, buffer, sems, source_of, target_of, dims, accumulator):
    def step(chunk, carry):
        first = chunk * UNROLL
        for part in range(UNROLL // LOAD):
            @pl.when(first + part * LOAD < count)
            def _():
                load_tiles(k, slab, chunk * (UNROLL // LOAD) + part, tiles, buffer, sems).wait()
        products, targets = [], []
        for j in range(0, UNROLL, 2):
            c = first + j
            pair = [meta[slab, c], meta[slab, c + 1]]
            left = jnp.concatenate([source_of(e) for e in pair], axis=0)
            right = jnp.concatenate([buffer[k, c], buffer[k, c + 1]], axis=0 if dims[1] == (1,) else 1)
            r = lax.dot_general(left, right, (dims, ((), ())), preferred_element_type=F32)
            rows = r.shape[0] // 2
            for i in range(2):
                part = r[i * rows:(i + 1) * rows, i * LANES:(i + 1) * LANES]
                products.append(jnp.where(c + i < count, part, 0.0))
                targets.append(target_of(pair[i]))
        for t, r in zip(targets, products):
            accumulator[t] = accumulator[t] + r
        return carry

    lax.fori_loop(0, (count + UNROLL - 1) // UNROLL, step, 0)


def cost(pieces, tiles):
    used = pieces * tiles.shape[1] // 2
    tile = tiles.shape[2]
    return pl.CostEstimate(
        flops=2 * used * 16 * tile * tile, transcendentals=0, bytes_accessed=used * tile * tile * 4
    )


def forward_kernel(hops, where, first, last, meta, *refs):
    refs = list(refs)
    pieces = len(hops)
    arrays = [refs.pop(0) for _ in range(1 + max(a for a, _ in where))]
    xs = [arrays[a] if i is None else arrays[a].at[i] for a, i in where]
    tiles = refs.pop(0)
    start = None if first else refs.pop(0)
    norm = refs.pop(0) if last else None
    out, buffer, sems, x_buffer, x_sems, acc = refs
    loads = []
    for k in range(pieces):
        slab = slab_id(meta, hops[k])
        load = pltpu.make_async_copy(xs[k], x_buffer.at[k], x_sems.at[k])
        load.start()
        loads.append(load)
        if k == 0 and not first:
            seed = pltpu.make_async_copy(start, acc, x_sems.at[pieces])
            seed.start()
        start_tiles(k, slab, meta[META_COUNTS, slab], tiles, buffer, sems)
    if first:
        for b in range(acc.shape[0]):
            acc[b] = jnp.zeros(acc.shape[1:], F32)
    else:
        seed.wait()
    for k in range(pieces):
        slab = slab_id(meta, hops[k])
        loads[k].wait()
        over_tiles(
            k, slab, meta[META_COUNTS, slab], meta, tiles, buffer, sems,
            lambda entry, k=k: x_buffer[k, entry & 63], lambda entry: entry >> 6, ((1,), (1,)), acc,
        )
    if last:
        per_peer = out.shape[1]
        for b in range(acc.shape[0]):
            out[b // per_peer, b % per_peer] = (norm[pl.ds(b, 1), :] * acc[b]).astype(BF16)
    else:
        save = pltpu.make_async_copy(acc, out, x_sems.at[pieces + 1])
        save.start()
        save.wait()


def forward_call(entries, meta, tiles, start, norm, peers):
    pieces = len(entries)
    first, last = start is None, norm is not None
    arrays, where = [], []
    for array, index, _ in entries:
        at = [i for i, other in enumerate(arrays) if other is array]
        if not at:
            arrays.append(array)
        where.append((at[0] if at else len(arrays) - 1, index))
    hops = [hop for _, _, hop in entries]
    shape = arrays[0].shape if entries[0][1] is None else arrays[0].shape[1:]
    args = [meta, *arrays, tiles]
    specs = [spec(SMEM)] + [spec(ANY)] * len(arrays) + [spec(HBM)]
    if not first:
        args.append(start)
        specs.append(spec(ANY))
    if last:
        args.append(norm)
        specs.append(spec(VMEM))
        out = jax.ShapeDtypeStruct((peers, shape[0] // peers, *shape[1:]), BF16)
    else:
        out = jax.ShapeDtypeStruct(shape, F32)
    return pl.pallas_call(
        functools.partial(forward_kernel, hops, where, first, last),
        out_shape=out, in_specs=specs, out_specs=spec(VMEM) if last else spec(ANY),
        scratch_shapes=[
            VMEM((pieces, *tiles.shape[1:]), BF16),
            pltpu.SemaphoreType.DMA((pieces, tiles.shape[1] // LOAD)),
            VMEM((pieces, *shape), BF16),
            pltpu.SemaphoreType.DMA((pieces + 2,)),
            VMEM(shape, F32),
        ],
        compiler_params=params(48), cost_estimate=cost(pieces, tiles), name="forward_tiles",
    )(*args)


def backward_kernel(hops, mode, meta, *refs):
    refs = list(refs)
    pieces = len(hops)
    added = mode != "swap"
    ys = refs.pop(0)
    tiles = refs.pop(0)
    adds = refs.pop(0) if added else None
    extra = refs.pop(0) if mode == "send" else None
    outs = [refs.pop(0) for _ in range(1 if mode == "swap" else pieces)]
    if mode == "swap":
        outs = [outs[0].at[k] for k in range(pieces)]
    buffer, sems, y_buffer, y_sem, acc, save_sems = refs[:6]
    if added:
        add_buffer, add_sems = refs[6:]
    load = pltpu.make_async_copy(ys, y_buffer, y_sem.at[0])
    load.start()
    seeds = []
    for k in range(pieces):
        slab = slab_id(meta, hops[k])
        start_tiles(k, slab, meta[META_COUNTS, slab], tiles, buffer, sems)
        if added:
            seed = pltpu.make_async_copy(adds.at[k], add_buffer.at[k], add_sems.at[k])
            seed.start()
            seeds.append(seed)
    blocks, rows = acc.shape[1], acc.shape[2]
    per_peer = blocks // ys.shape[0]
    per_tile = LANES // rows
    saves = []
    for k in range(pieces):
        slab = slab_id(meta, hops[k])
        if added:
            seeds[k].wait()
        for b in range(blocks):
            if added:
                acc[k, b] = add_buffer[k, b // per_tile, pl.ds((b % per_tile) * rows, rows), :].astype(F32)
            else:
                acc[k, b] = jnp.zeros(acc.shape[2:], F32)
        if k == 0:
            load.wait()

        def source_of(entry):
            d = entry >> 6
            return y_buffer[d // per_peer, d % per_peer]

        over_tiles(
            k, slab, meta[META_COUNTS, slab], meta, tiles, buffer, sems, source_of,
            lambda entry: entry & 63, ((1,), (0,)), acc.at[k],
        )
        if outs[k].dtype == F32:
            save = pltpu.make_async_copy(acc.at[k], outs[k], save_sems.at[k])
        else:
            held = buffer.at[k, pl.ds(0, outs[k].shape[0])]
            for b in range(blocks):
                held[b // per_tile, pl.ds((b % per_tile) * rows, rows), :] = acc[k, b].astype(BF16)
            if extra is not None:
                split(extra[...], held.at[blocks // per_tile])
            save = pltpu.make_async_copy(held, outs[k], save_sems.at[k])
        save.start()
        saves.append(save)
    for save in saves:
        save.wait()


def split(value, tile):
    high = value.astype(BF16)
    tile[0:value.shape[0], :] = high
    tile[value.shape[0]:2 * value.shape[0], :] = (value - high.astype(F32)).astype(BF16)


def joined(tile):
    half = tile.shape[0] // 2
    return tile[0:half, :].astype(F32) + tile[half:2 * half, :].astype(F32)


def backward_call(hops, mode, ys, blocks, meta, tiles, adds=None, extra=None):
    pieces = len(hops)
    rows = ys.shape[2]
    packed = (blocks * rows // LANES, LANES, LANES)
    more = (packed[0] + 1, LANES, LANES)
    args, specs = [meta, ys, tiles], [spec(SMEM), spec(ANY), spec(HBM)]
    if mode != "swap":
        args.append(adds)
        specs.append(spec(ANY))
    if mode == "swap":
        outs = jax.ShapeDtypeStruct((pieces, *packed), BF16)
    elif mode == "send":
        args.append(extra)
        specs.append(spec(VMEM))
        outs = [jax.ShapeDtypeStruct(more, BF16)] * pieces
    else:
        outs = [jax.ShapeDtypeStruct((blocks, rows, LANES), F32)] + [jax.ShapeDtypeStruct(packed, BF16)] * (pieces - 1)
    scratch = [
        VMEM((pieces, *tiles.shape[1:]), BF16),
        pltpu.SemaphoreType.DMA((pieces, tiles.shape[1] // LOAD)),
        VMEM(ys.shape, BF16),
        pltpu.SemaphoreType.DMA((1,)),
        VMEM((pieces, blocks, rows, LANES), F32),
        pltpu.SemaphoreType.DMA((pieces,)),
    ]
    if mode != "swap":
        scratch += [VMEM((pieces, *packed), BF16), pltpu.SemaphoreType.DMA((pieces,))]
    return pl.pallas_call(
        functools.partial(backward_kernel, hops, mode),
        out_shape=outs, in_specs=specs,
        out_specs=spec(ANY) if mode == "swap" else [spec(ANY)] * pieces, scratch_shapes=scratch,
        compiler_params=params(48), cost_estimate=cost(pieces, tiles), name="backward_tiles",
    )(*args)


def dense_kernel(place, agg, received, norm, back, sent):
    peers, blocks, feat_local = agg.shape[0], agg.shape[1], agg.shape[2]
    hid_local = sent.shape[2]
    halves = hid_local // feat_local
    weight = jnp.concatenate(
        [
            jnp.concatenate([received[g, blocks, pl.ds(h * feat_local, feat_local), :] for h in range(halves)], axis=1)
            for g in range(peers)
        ],
        axis=0,
    )
    bias_rows = []
    for g in range(peers):
        parts = received[g, blocks + 1].astype(F32)
        bias_rows.append((parts[0:1] + parts[1:2] + parts[2:3])[:, :hid_local])
    bias = jnp.concatenate(bias_rows, axis=1)
    bias = jnp.transpose(jnp.broadcast_to(bias, (8, bias.shape[1])))[:, 0:1]
    grad = jnp.zeros((peers * feat_local + 8, weight.shape[1]), F32)
    for b in range(blocks):
        agg_b = jnp.concatenate([agg[g, b] for g in range(peers)], axis=0)
        cot_b = jnp.concatenate([received[g, b] for g in range(peers)], axis=0).astype(F32)
        pre = lax.dot_general(weight, agg_b, (((0,), (0,)), ((), ())), preferred_element_type=F32) + bias
        sig = 1.0 / (1.0 + jnp.exp(-pre))
        hid = (pre * sig).astype(BF16)
        grad_pre = (cot_b * sig * (1.0 + pre * (1.0 - sig))).astype(BF16)
        back_b = jnp.dot(weight, grad_pre, preferred_element_type=F32)
        back_b = (norm[pl.ds(place[0] * blocks + b, 1), :] * back_b).astype(BF16)
        left = jnp.concatenate([agg_b, jnp.ones((8, LANES), BF16)], axis=0)
        grad = grad + lax.dot_general(left, grad_pre, (((1,), (1,)), ((), ())), preferred_element_type=F32)
        for g in range(peers):
            sent[g, b] = hid[g * hid_local:(g + 1) * hid_local]
            back[g, b] = back_b[g * feat_local:(g + 1) * feat_local]
    for g in range(peers):
        for source, slot in ((grad[g * feat_local:(g + 1) * feat_local], blocks), (grad[peers * feat_local:], blocks + 4)):
            high = source.astype(BF16).astype(F32)
            for i, part in enumerate((high, source - high)):
                part = jnp.concatenate([part[:, h * LANES:(h + 1) * LANES] for h in range(halves)], axis=0)
                part = part.astype(BF16)
                if slot == blocks + 4:
                    back[g, slot + i] = part
                else:
                    for h in range(halves):
                        back[g, slot + i * halves + h] = part[h * feat_local:(h + 1) * feat_local]


def collect_kernel(received, hidden):
    peers, per_peer = received.shape[0], received.shape[1]
    for b in range(peers * per_peer):
        hidden[:, pl.ds(b * LANES, LANES)] = received[b // per_peer, b % per_peer]


def weight_sums_kernel(back, sums):
    rows = back.shape[2]
    first = back.shape[1] - 6
    for i in range(2):
        total = jnp.zeros((rows, LANES), F32)
        for g in range(back.shape[0]):
            total = total + (back[g, first + i].astype(F32) + back[g, first + 2 + i].astype(F32))
        sums[i * rows:(i + 1) * rows] = total
        tail = jnp.zeros((rows, LANES), F32)
        for g in range(back.shape[0]):
            tail = tail + back[g, first + 4 + i].astype(F32)
        sums[(2 + i) * rows:(3 + i) * rows] = tail


def cross_kernel(own, down, up, far, out):
    last = out.shape[0] - 1
    for t in range(last):
        total = (own[t].astype(F32) + far[t].astype(F32)) + (down[t].astype(F32) + up[t].astype(F32))
        out[t] = total.astype(BF16)
    split((joined(own.at[last]) + joined(far.at[last])) + (joined(down.at[last]) + joined(up.at[last])), out.at[last])


def finish_with_scale(scale, place, kept, norm, down, up, far, sent, came, out, grad_weight, grad_bias):
    rows = kept.shape[1]
    per_tile = LANES // rows
    for b in range(kept.shape[0]):
        total = kept[b]
        for r in (down, up, far, came):
            total = total + r[b // per_tile, pl.ds((b % per_tile) * rows, rows), :].astype(F32)
        out[:, pl.ds(b * LANES, LANES)] = norm[pl.ds(b, 1), :] * total
    last = sent.shape[0] - 1
    sums = (joined(sent.at[last]) + joined(came.at[last])) * scale
    hid_local = grad_bias.shape[1]
    halves = grad_weight.shape[1] // LANES
    for h in range(halves):
        grad_weight[:, h * LANES:(h + 1) * LANES] = sums[h * rows:(h + 1) * rows]
    low = 2 * rows + 8 * halves
    bias = jnp.zeros((1, hid_local), F32)
    for h in range(halves):
        row = sums[2 * rows + 8 * h:2 * rows + 8 * h + 1] + sums[low + 8 * h:low + 8 * h + 1]
        for i in range(LANES // hid_local):
            here = place[0] == h * (LANES // hid_local) + i
            bias = jnp.where(here, row[:, i * hid_local:(i + 1) * hid_local], bias)
    grad_bias[...] = bias


def on_device(feats, tiles, dst_block, src_block, tile_counts, norm, weight, bias, cotangent):
    rows, feat_local = feats.shape
    tile = tiles.shape[-1]
    blocks = rows // tile
    hid_local = cotangent.shape[1]
    peers = lax.axis_size("feat")
    slabs = lax.axis_size("nodes")
    per_peer = blocks // peers
    slots = tiles.shape[2]
    own_tiles = tiles[0]
    norm_blocks = norm.reshape(blocks, tile)
    me = lax.axis_index("nodes").astype(jnp.int32)
    place = lax.axis_index("feat").astype(jnp.int32).reshape(1)
    meta = jnp.concatenate(
        [
            src_block[0] + 64 * dst_block[0],
            jnp.concatenate([tile_counts, tile_counts], axis=1),
            jnp.full((1, slots), me, jnp.int32),
        ],
        axis=0,
    )

    def move(value, dx, dy, dc):
        pairs = []
        for i in range(slabs):
            x, y, c = i // 8, (i // 2) % 4, i % 2
            pairs.append((i, ((x + dx) % 2) * 8 + ((y + dy) % 4) * 2 + (c + dc) % 2))
        return lax.ppermute(value, "nodes", pairs)

    scaled = pl.pallas_call(
        scale_kernel,
        out_shape=jax.ShapeDtypeStruct((blocks, feat_local, LANES), BF16),
        compiler_params=params(56), name="scale",
    )(feats.T, norm_blocks)
    payload = pl.pallas_call(
        payload_kernel,
        out_shape=jax.ShapeDtypeStruct((peers, per_peer + 2, hid_local, LANES), BF16),
        compiler_params=params(56), name="payload",
    )(cotangent.T, weight, bias.reshape(1, hid_local))
    across = move(scaled, 1, 0, 0)
    down, up = move(scaled, 0, 1, 0), move(scaled, 0, 3, 0)
    entries = [(scaled, None, (0, 0, 0)), (move(scaled, 0, 0, 1), None, (0, 0, 1))]
    across, down, up = lax.optimization_barrier((across, down, up))
    down_across, up_across = move(across, 0, 1, 0), move(across, 0, 3, 0)
    received = lax.all_to_all(payload, "feat", 0, 0)
    far, far_across, received = lax.optimization_barrier((scaled, across, received))
    far, far_across = move(far, 0, 2, 0), move(far_across, 0, 2, 0)

    def group(values, hops):
        moved = move(jnp.stack(values), 0, 0, 1)
        near = [(v, None, (*hop, 0)) for v, hop in zip(values, hops)]
        return near, [(moved, i, (*hop, 1)) for i, hop in enumerate(hops)]

    near, other = group([across, down, up], [(1, 0), (0, 3), (0, 1)])
    total = forward_call(entries + near + other, meta, own_tiles, None, None, peers)
    *values, total = lax.optimization_barrier((down_across, up_across, far, far_across, total))
    near, other = group(values, [(1, 3), (1, 1), (0, 2), (1, 2)])
    total = forward_call(near, meta, own_tiles, total, None, peers)
    total = forward_call(other, meta, own_tiles, total, norm_blocks, peers)
    agg = lax.all_to_all(total, "feat", 0, 0)
    back, sent = pl.pallas_call(
        dense_kernel,
        out_shape=(
            jax.ShapeDtypeStruct((peers, per_peer + 6, feat_local, LANES), BF16),
            jax.ShapeDtypeStruct((peers, per_peer, hid_local, LANES), BF16),
        ),
        in_specs=[spec(SMEM), spec(VMEM), spec(VMEM), spec(VMEM)],
        compiler_params=params(48), name="dense",
    )(place, agg, received, norm_blocks)
    back = lax.all_to_all(back, "feat", 0, 0)

    summed = pl.pallas_call(
        weight_sums_kernel,
        out_shape=jax.ShapeDtypeStruct((4 * feat_local, LANES), F32),
        compiler_params=params(), name="weight_sums",
    )(back)
    ways = [(0, 0), (0, 1), (0, 3), (0, 2)]
    over = [(1, dy) for _, dy in ways]
    mine = backward_call([(*hop, 1) for hop in over], "swap", back, blocks, meta, own_tiles)
    mine_too = backward_call([(*hop, 1) for hop in ways], "swap", after(back, mine), blocks, meta, own_tiles)
    swapped, mine_too, theirs = lax.optimization_barrier((move(mine, 0, 0, 1), mine_too, move(summed, 0, 0, 1)))
    sums = backward_call([(*hop, 0) for hop in over], "send", back, blocks, meta, own_tiles, swapped, summed + theirs)
    crossing = [move(p, *hop, 0) for p, hop in zip(sums[1:], ways[1:])]
    swapped = after(move(mine_too, 0, 0, 1), sums[1])
    parts = backward_call([(*hop, 0) for hop in ways], "keep", back, blocks, meta, own_tiles, swapped)
    arrived = [move(p, *hop, 0) for p, hop in zip(parts[1:], ways[1:])]
    *crossing, arrived[2] = lax.optimization_barrier((*crossing, arrived[2]))
    crossed = pl.pallas_call(
        cross_kernel,
        out_shape=jax.ShapeDtypeStruct(sums[0].shape, BF16),
        compiler_params=params(), name="cross",
    )(sums[0], *crossing)
    hidden = pl.pallas_call(
        collect_kernel,
        out_shape=jax.ShapeDtypeStruct((hid_local, rows), BF16),
        compiler_params=params(48), name="collect",
    )(lax.all_to_all(after(sent, parts[1]), "feat", 0, 0))
    came = move(crossed, 1, 0, 0)
    grad_feats, grad_weight, grad_bias = pl.pallas_call(
        functools.partial(finish_with_scale, float((rows * slabs) ** -0.5)),
        out_shape=(
            jax.ShapeDtypeStruct((feat_local, rows), F32),
            jax.ShapeDtypeStruct(weight.shape, F32),
            jax.ShapeDtypeStruct((1, hid_local), F32),
        ),
        in_specs=[spec(SMEM)] + [spec(VMEM)] * 7,
        compiler_params=params(), name="finish",
    )(after(place, hidden), parts[0], norm_blocks, *arrived, crossed, came)
    return hidden.T, grad_weight, grad_bias.reshape(hid_local), grad_feats.T


def solution(mesh):
    return jax.shard_map(
        on_device,
        mesh=mesh,
        in_specs=(
            P("nodes", "feat"),
            P("nodes", None, None, None, None),
            P("nodes", None, None),
            P("nodes", None, None),
            P("nodes", None),
            P("nodes"),
            P("feat", None),
            P("feat"),
            P("nodes", "feat"),
        ),
        out_specs=(P("nodes", "feat"), P("feat", None), P("feat"), P("nodes", "feat")),
        check_vma=False,
    )
```
